256 devices in a mesh: gx: 4 (over y), gy: 8 (over x, core), gz: 8 (over z).
Axes of the slice: x: 4, y: 4, z: 8, core: 2. Of those that a mesh axis runs over, the one named last changes fastest.
Arguments:
- density: float32 [128, 256, 1024], P('gx', 'gy', 'gz'), may hold values from -3.5 to 3.5
- conductance: float32 [3, 128, 256, 1024], P(None, 'gx', 'gy', 'gz'), may hold values from 0.25 to 1
- decay_rate: float32 [128, 256, 1024], P('gx', 'gy', 'gz'), may hold values from 0.5 to 4
- diffusion_numbers: float32 [3], replicated, may hold values from 2 to 8
- plane_offset: int32 [1], replicated, may hold values from 0 to 1023
Outputs:
- updated: float32 [128, 256, 1024], P('gx', 'gy', 'gz')
The draws below stay inside these ranges and needn't reach their ends.
All inputs are finite; a program needn't handle non-finite values.
Results may differ from the reference program's by a relative error of at most 0.0011.
Values sent between devices are 32-bit elements; how exact they have to be, the bound alone decides.
A program may use at most 64 MiB of HBM per device.

```python
import math
import jax
import jax.numpy as jnp
from jax import lax

CX = 32
CY = 32
CZ = 128
NX = 128
NY = 256
NZ = 1024


def levels(stream_key, extent, split, low, largest):
    level, own = 1.0, jax.random.fold_in(stream_key, 6)
    for axis_at, blocks in split:
        heights = jnp.exp(jax.random.uniform(jax.random.fold_in(own, axis_at), (blocks,), jnp.float32, low / len(split), largest / len(split)))
        level = level * jnp.repeat(heights, extent[axis_at] // blocks).reshape([-1 if axis == axis_at else 1 for axis in range(len(extent))])
    return level


def scatter_about(key, extent, deviation, most, cuts=(), held_as=jnp.bfloat16):
    gain = levels(key, extent, cuts, -0.22, 0.18) if cuts else 1.0
    values = jax.random.normal(key, extent, jnp.float32) * deviation * gain
    return jnp.minimum(jnp.maximum(values, -most), most).astype(held_as)


def setup_inputs(seed: int = 0) -> dict:
    seeds = jax.random.split(jax.random.key(seed), 6)
    return {
        "density": scatter_about(seeds[0], (NX, NY, NZ), 0.7, 3.5, ((0, 4), (1, 8), (2, 8)), jnp.float32),
        "conductance": jnp.clip(jnp.exp(math.log(1.0) - 1.3862944 * jax.random.uniform(seeds[1], (3, NX, NY, NZ), jnp.float32) ** levels(seeds[1], (3, NX, NY, NZ), ((1, 4), (2, 8), (3, 8)), -0.2, 0.2)), 0.25, 1.0),
        "decay_rate": jnp.clip(jnp.exp(math.log(4.0) - 2.0794415 * jax.random.uniform(seeds[2], (NX, NY, NZ), jnp.float32) ** levels(seeds[2], (NX, NY, NZ), ((0, 4), (1, 8), (2, 8)), -0.2, 0.2)), 0.5, 4.0),
        "diffusion_numbers": jnp.clip(jnp.exp(jax.random.uniform(seeds[3], (3,), jnp.float32, math.log(2.0), math.log(8.0))), 2.0, 8.0),
        "plane_offset": jax.random.randint(seeds[4], (1,), 0, NZ).astype(jnp.int32),
    }


implicit_weight = 0.5


def tridiagonal_sweep(lower_band, main_band, upper_band, right_side):
    def forward(state_pair, row_items):
        prior_upper, prior_right = state_pair
        band_low, band_mid, band_up, band_rhs = row_items
        pivot_value = band_mid - band_low * prior_upper
        next_upper = band_up / pivot_value
        next_right = (band_rhs - band_low * prior_right) / pivot_value
        return (next_upper, next_right), (next_upper, next_right)

    start_pair = (jnp.zeros_like(lower_band[0]), jnp.zeros_like(right_side[0]))
    _, (uppers, rights) = lax.scan(forward, start_pair, (lower_band, main_band, upper_band, right_side))

    def backward(later_value, row_items):
        band_up, band_rhs = row_items
        new_value = band_rhs - band_up * later_value
        return new_value, new_value

    _, solved = lax.scan(backward, jnp.zeros_like(right_side[0]), (uppers, rights), reverse=True)
    return solved


def periodic_solve(lower_band, main_band, upper_band, right_side):
    corner = -main_band[0]
    first_low = lower_band[0]
    last_up = upper_band[-1]
    changed = main_band.at[0].add(-corner)
    changed = changed.at[-1].add(-first_low * last_up / corner)
    low_cut = lower_band.at[0].set(0.0)
    up_cut = upper_band.at[-1].set(0.0)
    column = jnp.zeros_like(right_side).at[0].set(corner)
    column = column.at[-1].set(last_up)
    pair_solve = tridiagonal_sweep(low_cut[:, None], changed[:, None], up_cut[:, None], jnp.stack([right_side, column], axis=1))
    primary = pair_solve[:, 0]
    secondary = pair_solve[:, 1]
    factor_ratio = (primary[0] + first_low * primary[-1] / corner) / (1.0 + secondary[0] + first_low * secondary[-1] / corner)
    return primary - factor_ratio * secondary


def to_lines(volume, axis_number):
    shifted_axes = jnp.moveaxis(volume, axis_number, 0)
    return shifted_axes.reshape(shifted_axes.shape[0], -1)


def from_lines(line_array, axis_number, full_shape):
    moved_shape = (full_shape[axis_number],) + tuple(full_shape[index_dim] for index_dim in range(3) if index_dim != axis_number)
    return jnp.moveaxis(line_array.reshape(moved_shape), 0, axis_number)


def reference(density, conductance, decay_rate, diffusion_numbers, plane_offset):
    cell_counts = (CX, CY, CZ)
    full_shape = density.shape
    flux_sum = jnp.zeros_like(density)
    for axis_number in range(3):
        scale_value = diffusion_numbers[axis_number] * float(cell_counts[axis_number] * cell_counts[axis_number])
        coupling = conductance[axis_number]
        next_cells = jnp.roll(density, -1, axis_number)
        prev_cells = jnp.roll(density, 1, axis_number)
        behind = jnp.roll(coupling, 1, axis_number)
        flux_sum = flux_sum + scale_value * (coupling * (next_cells - density) - behind * (density - prev_cells))
    z_index = jnp.arange(NZ, dtype=jnp.int32)
    phase_angle = ((z_index + plane_offset[0]) % NZ).astype(jnp.float32) * (2.0 * math.pi / NZ)
    forcing = 2.0 * jnp.sin(phase_angle)
    explicit = flux_sum - decay_rate * density * (1.0 + density * density) + forcing[None, None, :]
    stiffness = decay_rate * (1.0 + 3.0 * density * density)
    update = explicit
    for axis_number in range(3):
        scale_value = diffusion_numbers[axis_number] * float(cell_counts[axis_number] * cell_counts[axis_number])
        coupling = conductance[axis_number]
        lower_band = -implicit_weight * scale_value * jnp.roll(coupling, 1, axis_number)
        upper_band = -implicit_weight * scale_value * coupling
        main_band = 1.0 - lower_band - upper_band
        if axis_number == 0:
            main_band = main_band + implicit_weight * stiffness
        solved = periodic_solve(to_lines(lower_band, axis_number), to_lines(main_band, axis_number), to_lines(upper_band, axis_number), to_lines(update, axis_number))
        update = from_lines(solved, axis_number, full_shape)
    return density + update
```

```python
import functools
import math

import jax
import jax.numpy as jnp
from jax import lax
from jax.experimental import pallas as pl
from jax.experimental.pallas import tpu as pltpu
from jax.sharding import PartitionSpec as P

MESH = pl.DeviceIdType.MESH
F32 = jnp.float32
AXES = ("gx", "gy", "gz")
WEIGHT = 0.5


def far_first(n):
    return sorted(range(1, n), key=lambda j: (-min(j, n - j), j))


def rows_loop(lo, count, step, body, carry, unroll):
    whole = count // unroll

    def block(k, c):
        for m in range(unroll):
            c = body(lo + step * (k * unroll + m), c)
        return c

    carry = lax.fori_loop(0, whole, block, carry)
    for m in range(whole * unroll, count):
        carry = body(lo + step * m, carry)
    return carry


def eliminate(excess, coupling, left, e):
    inverse = 1.0 / (excess + coupling + e)
    alpha, beta, leak = e * inverse, coupling * inverse, excess * inverse
    return inverse, alpha, beta, e * leak, e * beta, left + coupling * leak


def ring_factors(nodes):
    n = len(nodes)
    total = [nodes[j][1] + nodes[j - 1][2] for j in range(n)]
    alphas, betas = {}, {}
    coupling, excess, leak1 = nodes[1][0], total[2], total[1]
    for j in range(2, n):
        _, alphas[j], betas[j], carried, coupling, leak1 = eliminate(excess, coupling, leak1, nodes[j][0])
        excess = carried + total[(j + 1) % n]
    leak0 = excess
    c = nodes[0][0] + coupling
    inverse = 1.0 / (leak0 * leak1 + c * (leak0 + leak1))
    to0, to1 = {}, {}
    p, q = jnp.zeros_like(c), jnp.ones_like(c)
    for j in reversed(range(2, n)):
        p, q = betas[j] + alphas[j] * p, alphas[j] * q
        to1[j], to0[j] = p, q
    return [to0[j] for j in range(2, n)] + [to1[j] for j in range(2, n)] + [(leak1 + c) * inverse, c * inverse, (leak0 + c) * inverse]


def ring_apply(factors, loads):
    n = len(loads)
    right = [loads[j][0] + loads[j - 1][1] for j in range(n)]
    sum0, sum1 = right[0], right[1]
    for j in range(2, n):
        sum0 = sum0 + factors(j - 2) * right[j]
        sum1 = sum1 + factors(n - 2 + j - 2) * right[j]
    g00, g01, g11 = (factors(2 * (n - 2) + k) for k in range(3))
    return g00 * sum0 + g01 * sum1, g01 * sum0 + g11 * sum1


def kernel(
    sizes,
    diff_ref, offset_ref, v_hbm, c_hbm, dec_hbm, out_hbm,
    vx, cx, cy, cz, dec, vy, cyy, vz, czz,
    ax, bx, rx, ay, by, ry, az, bz, rz, segz,
    wx, wy, wz, work1, work2, work3,
    halo_x, halo_y, halo_z,
    mx_own, my_own, mz_own, mx_in, my_in, mz_in,
    fx_own, fy_own, fz_own, fx_in, fy_in, fz_in,
    load_sem, halo_send, halo_recv, mat_send, mat_recv, rhs_send, rhs_recv, out_sem,
):
    me = [lax.axis_index(a) for a in AXES]

    def peer(axis, shift):
        n = sizes[axis]
        return {AXES[axis]: lax.rem(me[axis] + (shift % n), n)}

    loads = [
        pltpu.make_async_copy(src, dst, load_sem.at[k])
        for k, (src, dst) in enumerate(((v_hbm, vx), (c_hbm.at[2], cz), (c_hbm.at[1], cy), (c_hbm.at[0], cx), (dec_hbm, dec)))
    ]
    for copy in loads:
        copy.start()

    barrier = pltpu.get_barrier_semaphore()
    for axis in range(3):
        for j in far_first(sizes[axis]):
            pl.semaphore_signal(barrier, inc=1, device_id=peer(axis, j), device_id_type=MESH)

    def remote(src, dst, send, recv, axis, shift):
        return pltpu.make_async_remote_copy(
            src_ref=src, dst_ref=dst, send_sem=send, recv_sem=recv, device_id=peer(axis, shift), device_id_type=MESH
        )

    scale = [diff_ref[a] * float(c * c) for a, c in enumerate((32, 32, 128))]
    half = [WEIGHT * s for s in scale]

    vx2, cy2, cz2, vz2, czz2 = (ref.reshape(1024, 128) for ref in (vx, cy, cz, vz, czz))

    loads[0].wait()
    loads[1].wait()

    def to_y(y, _):
        for xc in range(4):
            vy[xc, y] = vx2[pl.ds(xc * 256 + y, 8, stride=32), :]
            work1[xc, y] = cz2[pl.ds(xc * 256 + y, 8, stride=32), :]
        return 0

    rows_loop(0, 32, 1, to_y, 0, 4)

    def into_z(src, dst2):
        for b in range(8):
            block = src[b // 2, pl.ds(16 * (b % 2), 16)].reshape(128, 128)
            dst2[pl.ds(b, 128, stride=8), :] = block.T

    into_z(vy, vz2)
    into_z(work1, czz2)

    pl.semaphore_wait(barrier, sum(sizes) - 3)

    halos = [
        remote(vx.at[0], halo_x, halo_send.at[0], halo_recv.at[0], 0, -1),
        remote(v_hbm.at[:, 0, 0, :], halo_y.at[0], halo_send.at[1], halo_recv.at[1], 1, -1),
        remote(v_hbm.at[:, 3, 7, :], halo_y.at[1], halo_send.at[2], halo_recv.at[2], 1, 1),
        remote(c_hbm.at[1, :, 3, 7, :], halo_y.at[2], halo_send.at[3], halo_recv.at[3], 1, 1),
        remote(vz.at[0, 0], halo_z.at[0], halo_send.at[4], halo_recv.at[4], 2, -1),
        remote(vz.at[3, 31], halo_z.at[1], halo_send.at[5], halo_recv.at[5], 2, 1),
        remote(czz.at[3, 31], halo_z.at[2], halo_send.at[6], halo_recv.at[6], 2, 1),
    ]
    for copy in halos:
        copy.start()

    for copy in loads[2:]:
        copy.wait()

    def to_y2(y, _):
        for xc in range(4):
            cyy[xc, y] = cy2[pl.ds(xc * 256 + y, 8, stride=32), :]
        return 0

    rows_loop(0, 32, 1, to_y2, 0, 4)

    def excess_x(i):
        v = vx[i]
        return 1.0 + WEIGHT * (dec[i] * (1.0 + 3.0 * (v * v)))

    def matrix_row(i, carry):
        (kx, lx, sx), (ky, ly, sy), (kz, lz, sz) = carry
        rx[i], ax[i], bx[i], cx_l, kx, sx = eliminate(excess_x(i) + lx, kx, sx, half[0] * cx[i])
        ry[:, i], ay[:, i], by[:, i], cy_l, ky, sy = eliminate(1.0 + ly, ky, sy, half[1] * cyy[:, i])
        rz[:, i], az[:, i], bz[:, i], cz_l, kz, sz = eliminate(1.0 + lz, kz, sz, half[2] * czz[:, i])
        return (kx, cx_l, sx), (ky, cy_l, sy), (kz, cz_l, sz)

    zero = jnp.zeros((4, 8, 128), F32)
    start = (
        (half[0] * cx[0], zero, excess_x(0)),
        (half[1] * cyy[:, 0], zero, zero + 1.0),
        (half[2] * czz[:, 0], zero, zero + 1.0),
    )
    ends = rows_loop(1, 31, 1, matrix_row, start, 1)
    for own, (coupling, carried, left) in zip((mx_own, my_own), ends[:2]):
        own[0], own[1], own[2] = coupling, left, carried
    kz, lz, sz = ends[2]
    coupling, left, excess = kz[0], sz[0], sz[1] + lz[0]
    for s in range(1, 4):
        inverse, alpha, beta, carried, coupling, left = eliminate(excess, coupling, left, kz[s])
        segz[0, s], segz[1, s], segz[2, s] = inverse, alpha, beta
        excess = carried + lz[s] + (sz[s + 1] if s < 3 else 0.0)
    mz_own[0], mz_own[1], mz_own[2] = coupling, left, excess

    mats, first = [], 0
    for axis, own, into in ((0, mx_own, mx_in), (1, my_own, my_in), (2, mz_own, mz_in)):
        for j in far_first(sizes[axis]):
            k = first + j - 1
            mats.append(remote(own, into.at[j - 1], mat_send.at[k], mat_recv.at[k], axis, -j))
            mats[-1].start()
        first += sizes[axis] - 1
    mats_of = (mats[: sizes[0] - 1], mats[sizes[0] - 1 : sizes[0] + sizes[1] - 2], mats[sizes[0] + sizes[1] - 2 :])

    for copy in halos:
        copy.wait()

    hy = halo_y.reshape(3, 4, 8, 128)

    def flux_y(y, carry):
        v, below = carry
        after = vy[:, y + 1]
        flux = scale[1] * (cyy[:, y] * (after - v))
        work1[:, y] = flux - below
        return after, flux

    v0 = vy[:, 0]
    v_last, below = rows_loop(0, 31, 1, flux_y, (v0, scale[1] * (hy[2] * (v0 - hy[1]))), 4)
    work1[:, 31] = scale[1] * (cyy[:, 31] * (hy[0] - v_last)) - below

    def flux_z(i, carry):
        v, below = carry
        after = vz[:, i + 1]
        flux = scale[2] * (czz[:, i] * (after - v))
        work2[:, i] = flux - below
        return after, flux

    v0 = vz[:, 0]
    c31, v31 = czz[:, 31], vz[:, 31]
    prev_v = jnp.concatenate([halo_z[1][None], v31[:3]], axis=0)
    prev_c = jnp.concatenate([halo_z[2][None], c31[:3]], axis=0)
    next_v = jnp.concatenate([v0[1:], halo_z[0][None]], axis=0)
    v_last, below = rows_loop(0, 31, 1, flux_z, (v0, scale[2] * (prev_c * (v0 - prev_v))), 4)
    work2[:, 31] = scale[2] * (c31 * (next_v - v_last)) - below

    def from_z(src, dst, plus):
        src2 = src.reshape(1024, 128)
        for b in range(8):
            at = (b // 2, pl.ds(16 * (b % 2), 16))
            dst[at] = plus[at] + src2[pl.ds(b, 128, stride=8), :].T.reshape(16, 8, 128)

    from_z(work2, work1, work1)

    lane = lax.broadcasted_iota(jnp.int32, (1, 8, 128), 2)
    length = 128 * sizes[2]
    phase = lax.rem(lane + (me[2] * 128 + offset_ref[0]), length).astype(F32) * (2.0 * math.pi / length)
    forcing = 2.0 * jnp.sin(phase)

    work1_2 = work1.reshape(1024, 128)

    def right_x(i, v, after, below):
        flux = scale[0] * (cx[i] * (after - v))
        base = (i // 8) * 256 + i % 8
        rest = jnp.stack([work1_2[pl.ds(base + 64 * yc, 8, stride=8), :] for yc in range(4)])
        right = (flux - below) + rest - dec[i] * v * (1.0 + v * v) + forcing
        return right, flux

    def forward_x(i, carry):
        v, below, y, load = carry
        after = vx[i + 1]
        right, flux = right_x(i, v, after, below)
        y = right + ax[i - 1] * y
        work3[i] = y
        return after, flux, y, load + bx[i] * y

    v0, v1, v2 = vx[0], vx[1], vx[2]
    load, flux = right_x(0, v0, v1, zero)
    y, flux = right_x(1, v1, v2, flux)
    work3[1] = y
    v, below, y, load = rows_loop(2, 29, 1, forward_x, (v2, flux, y, load + bx[1] * y), 1)
    right, flux = right_x(31, v, halo_x[...], below)
    y = right + ax[30] * y
    work3[31] = y
    fx_own[0] = load + bx[31] * y
    fx_own[1] = ax[31] * y - flux

    def exchange(axis, own, into, first):
        copies = []
        for j in far_first(sizes[axis]):
            k = first + j - 1
            copies.append(remote(own, into.at[j - 1], rhs_send.at[k], rhs_recv.at[k], axis, -j))
            copies[-1].start()
        return copies

    def factors(axis, own, into, weights):
        for copy in mats_of[axis]:
            copy.wait_recv()
        nodes = [tuple(own[k] for k in range(3))] + [tuple(into[j, k] for k in range(3)) for j in range(sizes[axis] - 1)]
        for k, value in enumerate(ring_factors(nodes)):
            weights[k] = value

    def solve(axis, own, into, weights, copies):
        for copy in copies:
            copy.wait_recv()
        pairs = [(own[0], own[1])] + [(into[j, 0], into[j, 1]) for j in range(sizes[axis] - 1)]
        return ring_apply(lambda k: weights[k], pairs)

    sent_x = exchange(0, fx_own, fx_in, 0)
    factors(0, mx_own, mx_in, wx)
    factors(1, my_own, my_in, wy)
    factors(2, mz_own, mz_in, wz)
    node, after = solve(0, fx_own, fx_in, wx, sent_x)

    work1x = work1.reshape(32, 4, 8, 128)
    u = after

    def backward_x(i, u):
        u = (rx[i] * work3[i] + bx[i] * node) + ax[i] * u
        work1x[i] = u
        return u

    rows_loop(31, 31, -1, backward_x, u, 2)
    work1x[0] = node

    def right_y(y):
        return jnp.stack([work1_2[pl.ds(xc * 256 + y, 8, stride=32), :] for xc in range(4)])

    def forward_y(i, carry):
        y, load = carry
        y = right_y(i) + ay[:, i - 1] * y
        work2[:, i] = y
        return y, load + by[:, i] * y

    y = right_y(1)
    work2[:, 1] = y
    y, load = rows_loop(2, 30, 1, forward_y, (y, right_y(0) + by[:, 1] * y), 2)
    fy_own[0] = load
    fy_own[1] = ay[:, 31] * y

    sent_y = exchange(1, fy_own, fy_in, sizes[0] - 1)
    node_y, after_y = solve(1, fy_own, fy_in, wy, sent_y)

    def backward_y(i, u):
        u = (ry[:, i] * work2[:, i] + by[:, i] * node_y) + ay[:, i] * u
        work1[:, i] = u
        return u

    rows_loop(31, 31, -1, backward_y, after_y, 2)
    work1[:, 0] = node_y

    into_z(work1, work2.reshape(1024, 128))

    def forward_z(i, carry):
        y, load = carry
        y = work2[:, i] + az[:, i - 1] * y
        work3z[:, i] = y
        return y, load + bz[:, i] * y

    work3z = work3.reshape(4, 32, 8, 128)
    y = work2[:, 1]
    work3z[:, 1] = y
    y, load = rows_loop(2, 30, 1, forward_z, (y, work2[:, 0] + bz[:, 1] * y), 2)
    carried = az[:, 31] * y
    ys, left = [None], load[0]
    for s in range(1, 4):
        y = load[s] + carried[s - 1]
        if s > 1:
            y = y + segz[1, s - 1] * ys[-1]
        ys.append(y)
        left = left + segz[2, s] * y
    fz_own[0] = left
    fz_own[1] = carried[3] + segz[1, 3] * ys[3]

    sent_z = exchange(2, fz_own, fz_in, sizes[0] + sizes[1] - 2)
    node_z, after_z = solve(2, fz_own, fz_in, wz, sent_z)
    ends_z = [after_z]
    for s in (3, 2, 1):
        ends_z.insert(0, (segz[0, s] * ys[s] + segz[2, s] * node_z) + segz[1, s] * ends_z[0])
    starts_z = jnp.stack([node_z] + ends_z[:3])

    def backward_z(i, u):
        u = (rz[:, i] * work3z[:, i] + bz[:, i] * starts_z) + az[:, i] * u
        work2[:, i] = u
        return u

    rows_loop(31, 31, -1, backward_z, jnp.stack(ends_z), 2)
    work2[:, 0] = starts_z

    from_z(work2, work1, vy)

    def to_x(y, _):
        for xc in range(4):
            vx2[pl.ds(xc * 256 + y, 8, stride=32), :] = work1[xc, y]
        return 0

    for copy in mats + sent_x + sent_y + sent_z:
        copy.wait_send()
    rows_loop(0, 32, 1, to_x, 0, 4)
    out = pltpu.make_async_copy(vx, out_hbm, out_sem)
    out.start()
    out.wait()


def on_device(sizes, density, conductance, decay_rate, diffusion_numbers, plane_offset):
    nx, ny, nz = sizes
    grid = (32, 4, 8, 128)
    lines = (4, 32, 8, 128)
    one = (4, 8, 128)
    peers = nx + ny + nz - 3
    vmem = lambda *shape: pltpu.VMEM(shape, F32)
    dma = lambda n: pltpu.SemaphoreType.DMA((n,))
    anywhere = pl.BlockSpec(memory_space=pl.ANY)
    scalar = pl.BlockSpec(memory_space=pltpu.SMEM)
    updated = pl.pallas_call(
        functools.partial(kernel, sizes),
        out_shape=jax.ShapeDtypeStruct(grid, F32),
        in_specs=[scalar, scalar, anywhere, anywhere, anywhere],
        out_specs=anywhere,
        scratch_shapes=[vmem(*grid)] * 5
        + [vmem(*lines)] * 4
        + [vmem(*grid)] * 3
        + [vmem(*lines)] * 6
        + [vmem(3, 4, 8, 128)]
        + [vmem(2 * nx - 1, *one), vmem(2 * ny - 1, *one), vmem(2 * nz - 1, 8, 128)]
        + [vmem(*lines), vmem(*lines), vmem(*grid)]
        + [vmem(*one), vmem(3, 32, 128), vmem(3, 8, 128)]
        + [vmem(3, *one), vmem(3, *one), vmem(3, 8, 128)]
        + [vmem(nx - 1, 3, *one), vmem(ny - 1, 3, *one), vmem(nz - 1, 3, 8, 128)]
        + [vmem(2, *one), vmem(2, *one), vmem(2, 8, 128)]
        + [vmem(nx - 1, 2, *one), vmem(ny - 1, 2, *one), vmem(nz - 1, 2, 8, 128)]
        + [dma(5), dma(7), dma(7), dma(peers), dma(peers), dma(peers), dma(peers), pltpu.SemaphoreType.DMA],
        compiler_params=pltpu.CompilerParams(collective_id=0, has_side_effects=True, vmem_limit_bytes=48 * 1024 * 1024),
        name="adi_step",
    )(
        diffusion_numbers,
        plane_offset,
        density.reshape(grid),
        conductance.reshape((3,) + grid),
        decay_rate.reshape(grid),
    )
    return updated.reshape(density.shape)


def solution(mesh):
    sizes = tuple(mesh.shape[a] for a in AXES)
    placed = (P("gx", "gy", "gz"), P(None, "gx", "gy", "gz"), P("gx", "gy", "gz"), P(), P())
    return jax.shard_map(
        functools.partial(on_device, sizes), mesh=mesh, in_specs=placed, out_specs=P("gx", "gy", "gz"), check_vma=False
    )
```

```python
import functools
import math

import jax
import jax.numpy as jnp
from jax import lax
from jax.experimental import pallas as pl
from jax.experimental.pallas import tpu as pltpu
from jax.sharding import PartitionSpec as P

MESH = pl.DeviceIdType.MESH
F32 = jnp.float32
AXES = ("gx", "gy", "gz")
WEIGHT = 0.5


def far_first(n):
    return sorted(range(1, n), key=lambda j: (-min(j, n - j), j))


def rows_loop(lo, count, step, body, carry, unroll):
    whole = count // unroll

    def block(k, c):
        for m in range(unroll):
            c = body(lo + step * (k * unroll + m), c)
        return c

    carry = lax.fori_loop(0, whole, block, carry)
    for m in range(whole * unroll, count):
        carry = body(lo + step * m, carry)
    return carry


def eliminate(excess, coupling, left, e):
    inverse = 1.0 / (excess + coupling + e)
    alpha, beta, leak = e * inverse, coupling * inverse, excess * inverse
    return inverse, alpha, beta, e * leak, e * beta, left + coupling * leak


def ring_factors(nodes):
    n = len(nodes)
    total = [nodes[j][1] + nodes[j - 1][2] for j in range(n)]
    alphas, betas = {}, {}
    coupling, excess, leak1 = nodes[1][0], total[2], total[1]
    for j in range(2, n):
        _, alphas[j], betas[j], carried, coupling, leak1 = eliminate(excess, coupling, leak1, nodes[j][0])
        excess = carried + total[(j + 1) % n]
    leak0 = excess
    c = nodes[0][0] + coupling
    inverse = 1.0 / (leak0 * leak1 + c * (leak0 + leak1))
    to0, to1 = {}, {}
    p, q = jnp.zeros_like(c), jnp.ones_like(c)
    for j in reversed(range(2, n)):
        p, q = betas[j] + alphas[j] * p, alphas[j] * q
        to1[j], to0[j] = p, q
    return [to0[j] for j in range(2, n)] + [to1[j] for j in range(2, n)] + [(leak1 + c) * inverse, c * inverse, (leak0 + c) * inverse]


def ring_apply(factors, loads):
    n = len(loads)
    right = [loads[j][0] + loads[j - 1][1] for j in range(n)]
    sum0, sum1 = right[0], right[1]
    for j in range(2, n):
        sum0 = sum0 + factors(j - 2) * right[j]
        sum1 = sum1 + factors(n - 2 + j - 2) * right[j]
    g00, g01, g11 = (factors(2 * (n - 2) + k) for k in range(3))
    return g00 * sum0 + g01 * sum1, g01 * sum0 + g11 * sum1


def kernel(
    sizes,
    diff_hbm, offset_hbm, v_hbm, c_hbm, dec_hbm, out,
    diff, offset, vx, cx, cy, cz, dec, vy, cyy, vz, czz,
    ax, bx, rx, ay, by, ry, az, bz, rz, segz,
    wx, wy, wz, work1, work2, work3,
    halo_x, halo_y, halo_z,
    mx_own, my_own, mz_own, mx_in, my_in, mz_in,
    fx_own, fy_own, fz_own, fx_in, fy_in, fz_in,
    load_sem, halo_send, halo_recv, mat_send, mat_recv, rhs_send, rhs_recv, known,
):
    me = [lax.axis_index(a) for a in AXES]

    def peer(axis, shift):
        n = sizes[axis]
        return {AXES[axis]: lax.rem(me[axis] + (shift % n), n)}

    def greet(sem, axes):
        for axis in axes:
            for shift in (-1, 1):
                pl.semaphore_signal(sem, inc=1, device_id=peer(axis, shift), device_id_type=MESH)

    def remote(src, dst, send, recv, axis, shift):
        return pltpu.make_async_remote_copy(
            src_ref=src, dst_ref=dst, send_sem=send, recv_sem=recv, device_id=peer(axis, shift), device_id_type=MESH
        )

    barrier = pltpu.get_barrier_semaphore()
    greet(barrier, (0, 1, 2))

    loads = [
        pltpu.make_async_copy(src, dst, load_sem.at[k])
        for k, (src, dst) in enumerate(
            ((v_hbm, vx), (c_hbm.at[2], cz), (diff_hbm, diff), (c_hbm.at[1], cy), (c_hbm.at[0], cx), (dec_hbm, dec), (offset_hbm, offset))
        )
    ]
    for copy in loads:
        copy.start()

    vx2, cy2, cz2, vz2, czz2 = (ref.reshape(1024, 128) for ref in (vx, cy, cz, vz, czz))
    work1_2, work2_2, out2 = (ref.reshape(1024, 128) for ref in (work1, work2, out))

    def into_z(src2, dst2, blocks):
        for b in blocks:
            dst2[pl.ds(b, 128, stride=8), :] = src2[pl.ds(128 * b, 128), :].T

    pl.semaphore_wait(barrier, 6)
    greet(known.at[0], (0, 1, 2))
    halos = [
        remote(v_hbm.at[:, 0, 0, :], halo_y.at[0], halo_send.at[1], halo_recv.at[1], 1, -1),
        remote(v_hbm.at[:, 3, 7, :], halo_y.at[1], halo_send.at[2], halo_recv.at[2], 1, 1),
        remote(c_hbm.at[1, :, 3, 7, :], halo_y.at[2], halo_send.at[3], halo_recv.at[3], 1, 1),
        remote(v_hbm.at[0], halo_x, halo_send.at[0], halo_recv.at[0], 0, -1),
    ]
    for copy in halos:
        copy.start()

    loads[0].wait()
    into_z(vx2, vz2, range(8))
    loads[1].wait()
    into_z(cz2, czz2, range(8))
    halos_z = [
        remote(vz.at[0, 0], halo_z.at[0], halo_send.at[4], halo_recv.at[4], 2, -1),
        remote(vz.at[3, 31], halo_z.at[1], halo_send.at[5], halo_recv.at[5], 2, 1),
        remote(czz.at[3, 31], halo_z.at[2], halo_send.at[6], halo_recv.at[6], 2, 1),
    ]
    for copy in halos_z:
        copy.start()
    pl.semaphore_wait(known.at[0], 6)
    greet(known.at[1], (1, 2))

    for copy in loads[2:]:
        copy.wait()
    scale = [diff[a] * float(c * c) for a, c in enumerate((32, 32, 128))]
    half = [WEIGHT * s for s in scale]

    def to_y(y, _):
        for xc in range(4):
            at = pl.ds(xc * 256 + y, 8, stride=32)
            vy[xc, y] = vx2[at, :]
            cyy[xc, y] = cy2[at, :]
        return 0

    rows_loop(0, 32, 1, to_y, 0, 4)

    def excess_x(i):
        v = vx[i]
        return 1.0 + WEIGHT * (dec[i] * (1.0 + 3.0 * (v * v)))

    def matrix_row(i, carry):
        (kx, lx, sx), (ky, ly, sy), (kz, lz, sz) = carry
        rx[i], ax[i], bx[i], cx_l, kx, sx = eliminate(excess_x(i) + lx, kx, sx, half[0] * cx[i])
        ry[:, i], ay[:, i], by[:, i], cy_l, ky, sy = eliminate(1.0 + ly, ky, sy, half[1] * cyy[:, i])
        rz[:, i], az[:, i], bz[:, i], cz_l, kz, sz = eliminate(1.0 + lz, kz, sz, half[2] * czz[:, i])
        return (kx, cx_l, sx), (ky, cy_l, sy), (kz, cz_l, sz)

    zero = jnp.zeros((4, 8, 128), F32)
    start = (
        (half[0] * cx[0], zero, excess_x(0)),
        (half[1] * cyy[:, 0], zero, zero + 1.0),
        (half[2] * czz[:, 0], zero, zero + 1.0),
    )
    ends = rows_loop(1, 31, 1, matrix_row, start, 1)
    for own, (coupling, carried, left) in zip((mx_own, my_own), ends[:2]):
        own[0], own[1], own[2] = coupling, left, carried
    kz, lz, sz = ends[2]
    coupling, left, excess = kz[0], sz[0], sz[1] + lz[0]
    for s in range(1, 4):
        inverse, alpha, beta, carried, coupling, left = eliminate(excess, coupling, left, kz[s])
        segz[0, s], segz[1, s], segz[2, s] = inverse, alpha, beta
        excess = carried + lz[s] + (sz[s + 1] if s < 3 else 0.0)
    mz_own[0], mz_own[1], mz_own[2] = coupling, left, excess

    def send_matrix(axis, own, into, first, near, far):
        copies = []
        for j in far_first(sizes[axis]):
            if near <= min(j, sizes[axis] - j) <= far:
                k = first + j - 1
                copies.append(remote(own, into.at[j - 1], mat_send.at[k], mat_recv.at[k], axis, -j))
                copies[-1].start()
        return copies

    pl.semaphore_wait(known.at[1], 4)
    greet(known.at[2], (1, 2))
    first_y = sizes[0] - 1
    first_z = first_y + sizes[1] - 1
    mats_x = send_matrix(0, mx_own, mx_in, 0, 1, 2)
    mats_y = send_matrix(1, my_own, my_in, first_y, 1, 3)
    mats_z = send_matrix(2, mz_own, mz_in, first_z, 1, 3)

    halos = halos + halos_z
    for copy in halos:
        copy.wait()

    hy = halo_y.reshape(3, 4, 8, 128)

    def store_y(y, value):
        for xc in range(4):
            work1_2[pl.ds(xc * 256 + y, 8, stride=32), :] = value[xc]

    def flux_y(y, carry):
        v, below = carry
        after = vy[:, y + 1]
        flux = scale[1] * (cyy[:, y] * (after - v))
        store_y(y, flux - below)
        return after, flux

    v0 = vy[:, 0]
    v_last, below = rows_loop(0, 31, 1, flux_y, (v0, scale[1] * (hy[2] * (v0 - hy[1]))), 4)
    store_y(31, scale[1] * (cyy[:, 31] * (hy[0] - v_last)) - below)

    def flux_z(i, carry):
        v, below = carry
        after = vz[:, i + 1]
        flux = scale[2] * (czz[:, i] * (after - v))
        work2[:, i] = flux - below
        return after, flux

    v0 = vz[:, 0]
    c31, v31 = czz[:, 31], vz[:, 31]
    prev_v = jnp.concatenate([halo_z[1][None], v31[:3]], axis=0)
    prev_c = jnp.concatenate([halo_z[2][None], c31[:3]], axis=0)
    next_v = jnp.concatenate([v0[1:], halo_z[0][None]], axis=0)
    v_last, below = rows_loop(0, 31, 1, flux_z, (v0, scale[2] * (prev_c * (v0 - prev_v))), 4)
    work2[:, 31] = scale[2] * (c31 * (next_v - v_last)) - below

    for b in range(8):
        at = pl.ds(128 * b, 128)
        work1_2[at, :] = work1_2[at, :] + work2_2[pl.ds(b, 128, stride=8), :].T

    lane = lax.broadcasted_iota(jnp.int32, (1, 8, 128), 2)
    length = 128 * sizes[2]
    phase = lax.rem(lane + (me[2] * 128 + offset[0]), length).astype(F32) * (2.0 * math.pi / length)
    forcing = 2.0 * jnp.sin(phase)

    def exchange(axis, own, into, first):
        copies = []
        for j in far_first(sizes[axis]):
            k = first + j - 1
            copies.append(remote(own, into.at[j - 1], rhs_send.at[k], rhs_recv.at[k], axis, -j))
            copies[-1].start()
        return copies

    def factors(axis, own, into, weights, copies):
        for copy in copies:
            copy.wait_recv()
        nodes = [tuple(own[k] for k in range(3))] + [tuple(into[j, k] for k in range(3)) for j in range(sizes[axis] - 1)]
        for k, value in enumerate(ring_factors(nodes)):
            weights[k] = value

    def solve(axis, own, into, weight, copies):
        for copy in copies:
            copy.wait_recv()
        pairs = [(own[0], own[1])] + [(into[j, 0], into[j, 1]) for j in range(sizes[axis] - 1)]
        return ring_apply(weight, pairs)

    halves = [slice(2 * c, 2 * c + 2) for c in range(2)]
    sent_x = []
    for c, at in enumerate(halves):

        def right_x(i, v, after, below):
            flux = scale[0] * (cx[i, at] * (after - v))
            right = (flux - below) + work1[i, at] - dec[i, at] * v * (1.0 + v * v) + forcing
            return right, flux

        def forward_x(i, carry):
            v, below, y, load = carry
            after = vx[i + 1, at]
            right, flux = right_x(i, v, after, below)
            y = right + ax[i - 1, at] * y
            work3[i, at] = y
            return after, flux, y, load + bx[i, at] * y

        v0, v1, v2 = vx[0, at], vx[1, at], vx[2, at]
        load, flux = right_x(0, v0, v1, 0.0)
        y, flux = right_x(1, v1, v2, flux)
        work3[1, at] = y
        v, below, y, load = rows_loop(2, 29, 1, forward_x, (v2, flux, y, load + bx[1, at] * y), 2)
        right, flux = right_x(31, v, halo_x[at], below)
        y = right + ax[30, at] * y
        work3[31, at] = y
        fx_own[c, 0] = load + bx[31, at] * y
        fx_own[c, 1] = ax[31, at] * y - flux
        sent_x.append(exchange(0, fx_own.at[c], fx_in.at[c], c * (sizes[0] - 1)))

    pl.semaphore_wait(known.at[2], 4)
    mats_y += send_matrix(1, my_own, my_in, first_y, 4, 4)
    mats_z += send_matrix(2, mz_own, mz_in, first_z, 4, 4)
    factors(0, mx_own, mx_in, wx, mats_x)

    for c, at in enumerate(halves):
        node, after = solve(0, fx_own.at[c], fx_in.at[c], lambda k: wx[k, at], sent_x[c])

        def backward_x(i, u):
            u = (rx[i, at] * work3[i, at] + bx[i, at] * node) + ax[i, at] * u
            work1[i, at] = u
            return u

        rows_loop(31, 31, -1, backward_x, after, 4)
        work1[0, at] = node

    def right_y(y):
        return jnp.stack([work1_2[pl.ds(xc * 256 + y, 8, stride=32), :] for xc in range(4)])

    def forward_y(i, carry):
        y, load = carry
        y = right_y(i) + ay[:, i - 1] * y
        work2[:, i] = y
        return y, load + by[:, i] * y

    y = right_y(1)
    work2[:, 1] = y
    y, load = rows_loop(2, 30, 1, forward_y, (y, right_y(0) + by[:, 1] * y), 3)
    carried = ay[:, 31] * y
    sent_y, first = [], 2 * (sizes[0] - 1)
    for c, at in enumerate(halves):
        fy_own[c, 0] = load[at]
        fy_own[c, 1] = carried[at]
        sent_y.append(exchange(1, fy_own.at[c], fy_in.at[c], first))
        first += sizes[1] - 1

    factors(1, my_own, my_in, wy, mats_y)
    factors(2, mz_own, mz_in, wz, mats_z)

    zwork = work3.reshape(4, 32, 8, 128)
    zwork2 = work3.reshape(1024, 128)
    for c, at in enumerate(halves):
        node, after = solve(1, fy_own.at[c], fy_in.at[c], lambda k: wy[k, at], sent_y[c])

        def store_half(y, value):
            for m in range(2):
                work1_2[pl.ds((2 * c + m) * 256 + y, 8, stride=32), :] = value[m]

        def backward_y(i, u):
            u = (ry[at, i] * work2[at, i] + by[at, i] * node) + ay[at, i] * u
            store_half(i, u)
            return u

        rows_loop(31, 31, -1, backward_y, after, 4)
        store_half(0, node)
        into_z(work1_2, zwork2, range(4 * c, 4 * c + 4))

    def forward_z(i, carry):
        y, load = carry
        y = zwork[:, i] + az[:, i - 1] * y
        work2[:, i] = y
        return y, load + bz[:, i] * y

    y = zwork[:, 1]
    work2[:, 1] = y
    y, load = rows_loop(2, 30, 1, forward_z, (y, zwork[:, 0] + bz[:, 1] * y), 3)
    carried = az[:, 31] * y
    ys, left = [None], load[0]
    for s in range(1, 4):
        y = load[s] + carried[s - 1]
        if s > 1:
            y = y + segz[1, s - 1] * ys[-1]
        ys.append(y)
        left = left + segz[2, s] * y
    fz_own[0] = left
    fz_own[1] = carried[3] + segz[1, 3] * ys[3]

    sent_z = exchange(2, fz_own, fz_in, first)
    node, after = solve(2, fz_own, fz_in, lambda k: wz[k], sent_z)
    ends_z = [after]
    for s in (3, 2, 1):
        ends_z.insert(0, (segz[0, s] * ys[s] + segz[2, s] * node) + segz[1, s] * ends_z[0])
    starts_z = jnp.stack([node] + ends_z[:3])

    def backward_z(i, u):
        u = (rz[:, i] * work2[:, i] + bz[:, i] * starts_z) + az[:, i] * u
        zwork[:, i] = u
        return u

    rows_loop(31, 31, -1, backward_z, jnp.stack(ends_z), 4)
    zwork[:, 0] = starts_z

    for b in range(8):
        at = pl.ds(128 * b, 128)
        out2[at, :] = vx2[at, :] + zwork2[pl.ds(b, 128, stride=8), :].T
    for copy in mats_x + mats_y + mats_z + sum(sent_x, []) + sum(sent_y, []) + sent_z:
        copy.wait_send()


def on_device(sizes, density, conductance, decay_rate, diffusion_numbers, plane_offset):
    nx, ny, nz = sizes
    grid = (32, 4, 8, 128)
    lines = (4, 32, 8, 128)
    one = (4, 8, 128)
    two = (2, 8, 128)
    peers = nx + ny + nz - 3
    vmem = lambda *shape: pltpu.VMEM(shape, F32)
    dma = lambda n: pltpu.SemaphoreType.DMA((n,))
    operands = (
        diffusion_numbers,
        plane_offset,
        density.reshape(grid),
        conductance.reshape((3,) + grid),
        decay_rate.reshape(grid),
    )
    updated = pl.pallas_call(
        functools.partial(kernel, sizes),
        out_shape=jax.ShapeDtypeStruct(grid, F32),
        in_specs=[pl.BlockSpec(memory_space=pl.ANY)] * len(operands),
        out_specs=pl.BlockSpec(memory_space=pltpu.VMEM),
        scratch_shapes=[pltpu.SMEM((3,), F32), pltpu.SMEM((1,), jnp.int32)]
        + [vmem(*grid)] * 5
        + [vmem(*lines)] * 4
        + [vmem(*grid)] * 3
        + [vmem(*lines)] * 6
        + [vmem(3, 4, 8, 128)]
        + [vmem(2 * nx - 1, *one), vmem(2 * ny - 1, *one), vmem(2 * nz - 1, 8, 128)]
        + [vmem(*grid), vmem(*lines), vmem(*grid)]
        + [vmem(*one), vmem(3, 32, 128), vmem(3, 8, 128)]
        + [vmem(3, *one), vmem(3, *one), vmem(3, 8, 128)]
        + [vmem(nx - 1, 3, *one), vmem(ny - 1, 3, *one), vmem(nz - 1, 3, 8, 128)]
        + [vmem(2, 2, *two), vmem(2, 2, *two), vmem(2, 8, 128)]
        + [vmem(2, nx - 1, 2, *two), vmem(2, ny - 1, 2, *two), vmem(nz - 1, 2, 8, 128)]
        + [dma(7), dma(7), dma(7), dma(peers), dma(peers), dma(2 * peers), dma(2 * peers), pltpu.SemaphoreType.REGULAR((3,))],
        compiler_params=pltpu.CompilerParams(collective_id=0, has_side_effects=True, vmem_limit_bytes=40 * 1024 * 1024),
        name="adi_step",
    )(*(x if x.size == 1 else pltpu.with_memory_space_constraint(x, pltpu.MemorySpace.HBM) for x in operands))
    return updated.reshape(density.shape)


def solution(mesh):
    sizes = tuple(mesh.shape[a] for a in AXES)
    placed = (P("gx", "gy", "gz"), P(None, "gx", "gy", "gz"), P("gx", "gy", "gz"), P(), P())
    return jax.shard_map(
        functools.partial(on_device, sizes), mesh=mesh, in_specs=placed, out_specs=P("gx", "gy", "gz"), check_vma=False
    )
```

```python
import functools
import math

import jax
import jax.numpy as jnp
from jax import lax
from jax.experimental import pallas as pl
from jax.experimental.pallas import tpu as pltpu
from jax.sharding import PartitionSpec as P

MESH = pl.DeviceIdType.MESH
F32 = jnp.float32
AXES = ("gx", "gy", "gz")
WEIGHT = 0.5


def far_first(n):
    return sorted(range(1, n), key=lambda j: (-min(j, n - j), j))


def rows_loop(lo, count, step, body, carry, unroll):
    if unroll >= count:
        for m in range(count):
            carry = body(lo + step * m, carry)
        return carry
    whole = count // unroll

    def block(k, c):
        for m in range(unroll):
            c = body(lo + step * (k * unroll + m), c)
        return c

    carry = lax.fori_loop(0, whole, block, carry)
    for m in range(whole * unroll, count):
        carry = body(lo + step * m, carry)
    return carry


def eliminate(excess, coupling, left, e):
    inverse = 1.0 / (excess + coupling + e)
    alpha, beta, leak = e * inverse, coupling * inverse, excess * inverse
    return inverse, alpha, beta, e * leak, e * beta, left + coupling * leak


def ring_factors(nodes):
    n = len(nodes)
    total = [nodes[j][1] + nodes[j - 1][2] for j in range(n)]
    alphas, betas = {}, {}
    coupling, excess, leak1 = nodes[1][0], total[2], total[1]
    for j in range(2, n):
        _, alphas[j], betas[j], carried, coupling, leak1 = eliminate(excess, coupling, leak1, nodes[j][0])
        excess = carried + total[(j + 1) % n]
    leak0 = excess
    c = nodes[0][0] + coupling
    inverse = 1.0 / (leak0 * leak1 + c * (leak0 + leak1))
    to0, to1 = {}, {}
    p, q = jnp.zeros_like(c), jnp.ones_like(c)
    for j in reversed(range(2, n)):
        p, q = betas[j] + alphas[j] * p, alphas[j] * q
        to1[j], to0[j] = p, q
    return [to0[j] for j in range(2, n)] + [to1[j] for j in range(2, n)] + [(leak1 + c) * inverse, c * inverse, (leak0 + c) * inverse]


def ring_apply(factors, loads):
    n = len(loads)
    right = [loads[j][0] + loads[j - 1][1] for j in range(n)]
    sum0, sum1 = right[0], right[1]
    for j in range(2, n):
        sum0 = sum0 + factors(j - 2) * right[j]
        sum1 = sum1 + factors(n - 2 + j - 2) * right[j]
    g00, g01, g11 = (factors(2 * (n - 2) + k) for k in range(3))
    return g00 * sum0 + g01 * sum1, g01 * sum0 + g11 * sum1


def kernel(
    sizes,
    diff_hbm, offset_hbm, v_hbm, c_hbm, dec_hbm, out,
    diff, offset, vx, cx, cy, cz, dec, vy, cyy, czz,
    ax, bx, rx, ay, by, ry, az, bz, rz, segz,
    wx, wy, wz, work1, work2, work3,
    halo_x, halo_y, halo_z, edge, edge_rows, edge_fix,
    mx_own, my_own, mz_own, mx_in, my_in, mz_in,
    fx_own, fy_own, fz_own, fx_in, fy_in, fz_in,
    load_sem, halo_send, halo_recv, mat_send, mat_recv, rhs_send, rhs_recv, known,
):
    me = [lax.axis_index(a) for a in AXES]

    def peer(axis, shift):
        n = sizes[axis]
        return {AXES[axis]: lax.rem(me[axis] + (shift % n), n)}

    near = [(0, -1), (0, 1), (2, -1), (2, 1), (1, -1), (1, 1), (1, -2), (1, 2)]
    near_z = near[2:4]

    def greet(sem, peers):
        for axis, shift in peers:
            pl.semaphore_signal(sem, inc=1, device_id=peer(axis, shift), device_id_type=MESH)

    def remote(src, dst, send, recv, axis, shift):
        return pltpu.make_async_remote_copy(
            src_ref=src, dst_ref=dst, send_sem=send, recv_sem=recv, device_id=peer(axis, shift), device_id_type=MESH
        )

    barrier = pltpu.get_barrier_semaphore()
    greet(barrier, near)

    loads = [
        pltpu.make_async_copy(src, dst, load_sem.at[k])
        for k, (src, dst) in enumerate(
            ((v_hbm, vx), (c_hbm.at[2], cz), (diff_hbm, diff), (c_hbm.at[1], cy), (c_hbm.at[0], cx), (dec_hbm, dec), (offset_hbm, offset))
        )
    ]
    for copy in loads:
        copy.start()

    vx2, cy2, cz2, czz2 = (ref.reshape(1024, 128) for ref in (vx, cy, cz, czz))
    work1_2, work2_2, out2 = (ref.reshape(1024, 128) for ref in (work1, work2, out))

    def into_z(src2, dst2, blocks):
        for b in blocks:
            dst2[pl.ds(b, 128, stride=8), :] = src2[pl.ds(128 * b, 128), :].T

    lane = lax.broadcasted_iota(jnp.int32, (128, 128), 1)
    blocks = [pl.ds(128 * b, 128) for b in range(8)]
    loads[0].wait()
    packed = jnp.zeros((128, 128), F32)
    for b, at in enumerate(blocks):
        packed = jnp.where(lane // 2 == b, pltpu.roll(vx2[at, :], 2 * b + 1, 1), packed)
    loads[1].wait()
    for b, at in enumerate(blocks):
        packed = jnp.where(lane == 16 + b, pltpu.roll(cz2[at, :], 17 + b, 1), packed)
    edge_rows[...] = packed.T
    edge[0] = edge_rows[pl.ds(1, 8, stride=2), :]
    edge[1] = edge_rows[pl.ds(0, 8, stride=2), :]
    edge[2] = edge_rows[pl.ds(16, 8), :]

    pl.semaphore_wait(barrier, len(near))
    greet(known.at[0], near)
    halos = [
        remote(edge.at[0], halo_z.at[0], halo_send.at[4], halo_recv.at[4], 2, -1),
        remote(edge.at[1], halo_z.at[1], halo_send.at[5], halo_recv.at[5], 2, 1),
        remote(edge.at[2], halo_z.at[2], halo_send.at[6], halo_recv.at[6], 2, 1),
        remote(v_hbm.at[:, 0, 0, :], halo_y.at[0], halo_send.at[1], halo_recv.at[1], 1, -1),
        remote(v_hbm.at[:, 3, 7, :], halo_y.at[1], halo_send.at[2], halo_recv.at[2], 1, 1),
        remote(c_hbm.at[1, :, 3, 7, :], halo_y.at[2], halo_send.at[3], halo_recv.at[3], 1, 1),
        remote(v_hbm.at[0], halo_x, halo_send.at[0], halo_recv.at[0], 0, -1),
    ]
    for copy in halos:
        copy.start()

    for copy in loads[2:]:
        copy.wait()
    scale = [diff[a] * float(c * c) for a, c in enumerate((32, 32, 128))]
    half = [WEIGHT * s for s in scale]

    pl.semaphore_wait(known.at[0], len(near))
    greet(known.at[1], near_z)

    def to_y(y, _):
        for xc in range(4):
            at = pl.ds(xc * 256 + y, 8, stride=32)
            vy[xc, y] = vx2[at, :]
            cyy[xc, y] = cy2[at, :]
        return 0

    rows_loop(0, 32, 1, to_y, 0, 32)

    def excess_x(i):
        v = vx[i]
        return 1.0 + WEIGHT * (dec[i] * (1.0 + 3.0 * (v * v)))

    def matrix_row(i, carry):
        (kx, lx, sx), (ky, ly, sy) = carry
        rx[i], ax[i], bx[i], cx_l, kx, sx = eliminate(excess_x(i) + lx, kx, sx, half[0] * cx[i])
        ry[:, i], ay[:, i], by[:, i], cy_l, ky, sy = eliminate(1.0 + ly, ky, sy, half[1] * cyy[:, i])
        return (kx, cx_l, sx), (ky, cy_l, sy)

    zero = jnp.zeros((4, 8, 128), F32)
    start = (
        (half[0] * cx[0], zero, excess_x(0)),
        (half[1] * cyy[:, 0], zero, zero + 1.0),
    )
    ends = rows_loop(1, 31, 1, matrix_row, start, 32)
    for own, (coupling, carried, left) in zip((mx_own, my_own), ends):
        own[0], own[1], own[2] = coupling, left, carried
    def send_matrix(axis, own, into, first):
        copies = []
        for j in far_first(sizes[axis]):
            k = first + j - 1
            copies.append(remote(own, into.at[j - 1], mat_send.at[k], mat_recv.at[k], axis, -j))
            copies[-1].start()
        return copies

    first_y = sizes[0] - 1
    first_z = first_y + sizes[1] - 1
    mats_x = send_matrix(0, mx_own, mx_in, 0)
    mats_y = send_matrix(1, my_own, my_in, first_y)

    def at_y(y):
        return [pl.ds(xc * 256 + y, 8, stride=32) for xc in range(4)]

    def flux_y(y, carry):
        v, below = carry
        after = vy[:, y + 1]
        flux = scale[1] * (cyy[:, y] * (after - v))
        for xc, at in enumerate(at_y(y)):
            work1_2[at, :] = (flux - below)[xc]
        return after, flux

    v_last, below = rows_loop(0, 31, 1, flux_y, (vy[:, 0], zero), 32)
    for xc, at in enumerate(at_y(31)):
        work1_2[at, :] = -below[xc]
    for at in blocks:
        v = vx2[at, :]
        flux = jnp.where(lane < 127, scale[2] * (cz2[at, :] * (pltpu.roll(v, 127, 1) - v)), 0.0)
        work1_2[at, :] = work1_2[at, :] + (flux - pltpu.roll(flux, 1, 1))

    for copy in halos:
        copy.wait()

    hy = halo_y.reshape(3, 4, 8, 128)
    low = scale[1] * (hy[2] * (vy[:, 0] - hy[1]))
    high = scale[1] * (cyy[:, 31] * (hy[0] - v_last))
    for xc in range(4):
        at0, at31 = at_y(0)[xc], at_y(31)[xc]
        work1_2[at0, :] = work1_2[at0, :] - low[xc]
        work1_2[at31, :] = work1_2[at31, :] + high[xc]
    edge_fix[pl.ds(0, 8, stride=2), :] = scale[2] * (edge[2] * (halo_z[0] - edge[1]))
    edge_fix[pl.ds(1, 8, stride=2), :] = scale[2] * (halo_z[2] * (halo_z[1] - edge[0]))
    fix = jnp.concatenate([edge_fix[...], jnp.zeros((112, 128), F32)], axis=0).T
    outer = (lane == 0) | (lane == 127)
    for b, at in enumerate(blocks):
        work1_2[at, :] = work1_2[at, :] + jnp.where(outer, pltpu.roll(fix, 127 - 2 * b, 1), 0.0)

    z = lax.broadcasted_iota(jnp.int32, (1, 8, 128), 2)
    length = 128 * sizes[2]
    phase = lax.rem(z + (me[2] * 128 + offset[0]), length).astype(F32) * (2.0 * math.pi / length)
    forcing = 2.0 * jnp.sin(phase)

    def exchange(axis, own, into, first):
        copies = []
        for j in far_first(sizes[axis]):
            k = first + j - 1
            copies.append(remote(own, into.at[j - 1], rhs_send.at[k], rhs_recv.at[k], axis, -j))
            copies[-1].start()
        return copies

    def factors(axis, own, into, weights, copies):
        for copy in copies:
            copy.wait_recv()
        nodes = [tuple(own[k] for k in range(3))] + [tuple(into[j, k] for k in range(3)) for j in range(sizes[axis] - 1)]
        for k, value in enumerate(ring_factors(nodes)):
            weights[k] = value

    def solve(axis, own, into, weight, copies):
        for copy in copies:
            copy.wait_recv()
        pairs = [(own[0], own[1])] + [(into[j, 0], into[j, 1]) for j in range(sizes[axis] - 1)]
        return ring_apply(weight, pairs)

    halves = [slice(2 * c, 2 * c + 2) for c in range(2)]
    sent_x = []
    for c, at in enumerate(halves):

        def right_x(i, v, after, below):
            flux = scale[0] * (cx[i, at] * (after - v))
            right = (flux - below) + work1[i, at] - dec[i, at] * v * (1.0 + v * v) + forcing
            return right, flux

        def forward_x(i, carry):
            v, below, y, load = carry
            after = vx[i + 1, at]
            right, flux = right_x(i, v, after, below)
            y = right + ax[i - 1, at] * y
            work3[i, at] = y
            return after, flux, y, load + bx[i, at] * y

        v0, v1, v2 = vx[0, at], vx[1, at], vx[2, at]
        load, flux = right_x(0, v0, v1, 0.0)
        y, flux = right_x(1, v1, v2, flux)
        work3[1, at] = y
        v, below, y, load = rows_loop(2, 29, 1, forward_x, (v2, flux, y, load + bx[1, at] * y), 32)
        right, flux = right_x(31, v, halo_x[at], below)
        y = right + ax[30, at] * y
        work3[31, at] = y
        fx_own[c, 0] = load + bx[31, at] * y
        fx_own[c, 1] = ax[31, at] * y - flux
        sent_x.append(exchange(0, fx_own.at[c], fx_in.at[c], c * (sizes[0] - 1)))

    pl.semaphore_wait(known.at[1], len(near_z))
    greet(known.at[2], near_z)
    into_z(cz2, czz2, range(8))

    def matrix_row_z(i, carry):
        kz, lz, sz = carry
        rz[:, i], az[:, i], bz[:, i], lz, kz, sz = eliminate(1.0 + lz, kz, sz, half[2] * czz[:, i])
        return kz, lz, sz

    kz, lz, sz = rows_loop(1, 31, 1, matrix_row_z, (half[2] * czz[:, 0], zero, zero + 1.0), 32)
    coupling, left, excess = kz[0], sz[0], sz[1] + lz[0]
    for s in range(1, 4):
        inverse, alpha, beta, carried, coupling, left = eliminate(excess, coupling, left, kz[s])
        segz[0, s], segz[1, s], segz[2, s] = inverse, alpha, beta
        excess = carried + lz[s] + (sz[s + 1] if s < 3 else 0.0)
    mz_own[0], mz_own[1], mz_own[2] = coupling, left, excess

    pl.semaphore_wait(known.at[2], len(near_z))
    mats_z = send_matrix(2, mz_own, mz_in, first_z)
    factors(0, mx_own, mx_in, wx, mats_x)

    for c, at in enumerate(halves):
        node, after = solve(0, fx_own.at[c], fx_in.at[c], lambda k: wx[k, at], sent_x[c])

        def backward_x(i, u):
            u = (rx[i, at] * work3[i, at] + bx[i, at] * node) + ax[i, at] * u
            work1[i, at] = u
            return u

        rows_loop(31, 31, -1, backward_x, after, 32)
        work1[0, at] = node

    sent_y, first = [], 2 * (sizes[0] - 1)
    for c, at in enumerate(halves):

        def right_y(y):
            return jnp.stack([work1_2[pl.ds(xc * 256 + y, 8, stride=32), :] for xc in (2 * c, 2 * c + 1)])

        def forward_y(i, carry):
            y, load = carry
            y = right_y(i) + ay[at, i - 1] * y
            work2[at, i] = y
            return y, load + by[at, i] * y

        y = right_y(1)
        work2[at, 1] = y
        y, load = rows_loop(2, 30, 1, forward_y, (y, right_y(0) + by[at, 1] * y), 32)
        fy_own[c, 0] = load
        fy_own[c, 1] = ay[at, 31] * y
        sent_y.append(exchange(1, fy_own.at[c], fy_in.at[c], first))
        first += sizes[1] - 1

    factors(1, my_own, my_in, wy, mats_y)
    factors(2, mz_own, mz_in, wz, mats_z)

    zwork = work3.reshape(4, 32, 8, 128)
    zwork2 = work3.reshape(1024, 128)
    for c, at in enumerate(halves):
        node, after = solve(1, fy_own.at[c], fy_in.at[c], lambda k: wy[k, at], sent_y[c])

        def store_half(y, value):
            for m in range(2):
                work1_2[pl.ds((2 * c + m) * 256 + y, 8, stride=32), :] = value[m]

        def backward_y(i, u):
            u = (ry[at, i] * work2[at, i] + by[at, i] * node) + ay[at, i] * u
            store_half(i, u)
            return u

        rows_loop(31, 31, -1, backward_y, after, 32)
        store_half(0, node)
        into_z(work1_2, zwork2, range(4 * c, 4 * c + 4))

    def forward_z(i, carry):
        y, load = carry
        y = zwork[:, i] + az[:, i - 1] * y
        work2[:, i] = y
        return y, load + bz[:, i] * y

    y = zwork[:, 1]
    work2[:, 1] = y
    y, load = rows_loop(2, 30, 1, forward_z, (y, zwork[:, 0] + bz[:, 1] * y), 32)
    carried = az[:, 31] * y
    ys, left = [None], load[0]
    for s in range(1, 4):
        y = load[s] + carried[s - 1]
        if s > 1:
            y = y + segz[1, s - 1] * ys[-1]
        ys.append(y)
        left = left + segz[2, s] * y
    fz_own[0] = left
    fz_own[1] = carried[3] + segz[1, 3] * ys[3]

    sent_z = exchange(2, fz_own, fz_in, first)
    node, after = solve(2, fz_own, fz_in, lambda k: wz[k], sent_z)
    ends_z = [after]
    for s in (3, 2, 1):
        ends_z.insert(0, (segz[0, s] * ys[s] + segz[2, s] * node) + segz[1, s] * ends_z[0])
    starts_z = jnp.stack([node] + ends_z[:3])

    def backward_z(i, u):
        u = (rz[:, i] * work2[:, i] + bz[:, i] * starts_z) + az[:, i] * u
        zwork[:, i] = u
        return u

    rows_loop(31, 31, -1, backward_z, jnp.stack(ends_z), 32)
    zwork[:, 0] = starts_z

    for b in range(8):
        at = pl.ds(128 * b, 128)
        out2[at, :] = vx2[at, :] + zwork2[pl.ds(b, 128, stride=8), :].T
    for copy in mats_x + mats_y + mats_z + sum(sent_x, []) + sum(sent_y, []) + sent_z:
        copy.wait_send()


def on_device(sizes, density, conductance, decay_rate, diffusion_numbers, plane_offset):
    nx, ny, nz = sizes
    grid = (32, 4, 8, 128)
    lines = (4, 32, 8, 128)
    one = (4, 8, 128)
    two = (2, 8, 128)
    peers = nx + ny + nz - 3
    vmem = lambda *shape: pltpu.VMEM(shape, F32)
    dma = lambda n: pltpu.SemaphoreType.DMA((n,))
    operands = (
        diffusion_numbers,
        plane_offset,
        density.reshape(grid),
        conductance.reshape((3,) + grid),
        decay_rate.reshape(grid),
    )
    updated = pl.pallas_call(
        functools.partial(kernel, sizes),
        out_shape=jax.ShapeDtypeStruct(grid, F32),
        in_specs=[pl.BlockSpec(memory_space=pl.ANY)] * len(operands),
        out_specs=pl.BlockSpec(memory_space=pltpu.VMEM),
        scratch_shapes=[pltpu.SMEM((3,), F32), pltpu.SMEM((1,), jnp.int32)]
        + [vmem(*grid)] * 5
        + [vmem(*lines)] * 3
        + [vmem(*grid)] * 3
        + [vmem(*lines)] * 6
        + [vmem(3, 4, 8, 128)]
        + [vmem(2 * nx - 1, *one), vmem(2 * ny - 1, *one), vmem(2 * nz - 1, 8, 128)]
        + [vmem(*grid), vmem(*lines), vmem(*grid)]
        + [vmem(*one), vmem(3, 32, 128), vmem(3, 8, 128), vmem(3, 8, 128), vmem(128, 128), vmem(16, 128)]
        + [vmem(3, *one), vmem(3, *one), vmem(3, 8, 128)]
        + [vmem(nx - 1, 3, *one), vmem(ny - 1, 3, *one), vmem(nz - 1, 3, 8, 128)]
        + [vmem(2, 2, *two), vmem(2, 2, *two), vmem(2, 8, 128)]
        + [vmem(2, nx - 1, 2, *two), vmem(2, ny - 1, 2, *two), vmem(nz - 1, 2, 8, 128)]
        + [dma(7), dma(7), dma(7), dma(peers), dma(peers), dma(2 * peers), dma(2 * peers), pltpu.SemaphoreType.REGULAR((3,))],
        compiler_params=pltpu.CompilerParams(collective_id=0, has_side_effects=True, vmem_limit_bytes=40 * 1024 * 1024),
        name="adi_step",
    )(*(x if x.size == 1 else pltpu.with_memory_space_constraint(x, pltpu.MemorySpace.HBM) for x in operands))
    return updated.reshape(density.shape)


def solution(mesh):
    sizes = tuple(mesh.shape[a] for a in AXES)
    placed = (P("gx", "gy", "gz"), P(None, "gx", "gy", "gz"), P("gx", "gy", "gz"), P(), P())
    return jax.shard_map(
        functools.partial(on_device, sizes), mesh=mesh, in_specs=placed, out_specs=P("gx", "gy", "gz"), check_vma=False
    )
```

```python
import functools
import math

import jax
import jax.numpy as jnp
from jax import lax
from jax.experimental import pallas as pl
from jax.experimental.pallas import tpu as pltpu
from jax.sharding import PartitionSpec as P

MESH = pl.DeviceIdType.MESH
F32 = jnp.float32
AXES = ("gx", "gy", "gz")
WEIGHT = 0.5


def far_first(n):
    return sorted(range(1, n), key=lambda j: (-min(j, n - j), j))


def rows_loop(lo, count, step, body, carry, unroll):
    if unroll >= count:
        for m in range(count):
            carry = body(lo + step * m, carry)
        return carry
    whole = count // unroll

    def block(k, c):
        for m in range(unroll):
            c = body(lo + step * (k * unroll + m), c)
        return c

    carry = lax.fori_loop(0, whole, block, carry)
    for m in range(whole * unroll, count):
        carry = body(lo + step * m, carry)
    return carry


def eliminate(excess, coupling, left, e):
    inverse = 1.0 / (excess + coupling + e)
    alpha, beta, leak = e * inverse, coupling * inverse, excess * inverse
    return inverse, alpha, beta, e * leak, e * beta, left + coupling * leak


def ring_factors(nodes):
    n = len(nodes)
    total = [nodes[j][1] + nodes[j - 1][2] for j in range(n)]
    alphas, betas = {}, {}
    coupling, excess, leak1 = nodes[1][0], total[2], total[1]
    for j in range(2, n):
        _, alphas[j], betas[j], carried, coupling, leak1 = eliminate(excess, coupling, leak1, nodes[j][0])
        excess = carried + total[(j + 1) % n]
    leak0 = excess
    c = nodes[0][0] + coupling
    inverse = 1.0 / (leak0 * leak1 + c * (leak0 + leak1))
    to0, to1 = {}, {}
    p, q = jnp.zeros_like(c), jnp.ones_like(c)
    for j in reversed(range(2, n)):
        p, q = betas[j] + alphas[j] * p, alphas[j] * q
        to1[j], to0[j] = p, q
    return [to0[j] for j in range(2, n)] + [to1[j] for j in range(2, n)] + [(leak1 + c) * inverse, c * inverse, (leak0 + c) * inverse]


def ring_apply(factors, loads):
    n = len(loads)
    right = [loads[j][0] + loads[j - 1][1] for j in range(n)]
    sum0, sum1 = right[0], right[1]
    for j in range(2, n):
        sum0 = sum0 + factors(j - 2) * right[j]
        sum1 = sum1 + factors(n - 2 + j - 2) * right[j]
    g00, g01, g11 = (factors(2 * (n - 2) + k) for k in range(3))
    return g00 * sum0 + g01 * sum1, g01 * sum0 + g11 * sum1


def kernel(
    sizes,
    diff_hbm, offset_hbm, v_hbm, c_hbm, dec_hbm, out,
    diff, offset, vx, cx, cy, cz, dec, vy, cyy, czz,
    ax, bx, rx, ay, by, ry, az, bz, rz, segz,
    wx, wy, wz, work1, work2, work3,
    halo_x, halo_y, halo_z, edge, edge_rows, edge_fix,
    mx_own, my_own, mz_own, mx_in, my_in, mz_in,
    fx_own, fy_own, fz_own, fx_in, fy_in, fz_in,
    load_sem, halo_send, halo_recv, mat_send, mat_recv, rhs_send, rhs_recv, known,
):
    me = [lax.axis_index(a) for a in AXES]

    def peer(axis, shift):
        n = sizes[axis]
        return {AXES[axis]: lax.rem(me[axis] + (shift % n), n)}

    near = [(0, -1), (0, 1), (2, -1), (2, 1), (1, -1), (1, 1), (1, -2), (1, 2)]
    near_z = near[2:4]

    def greet(sem, peers):
        for axis, shift in peers:
            pl.semaphore_signal(sem, inc=1, device_id=peer(axis, shift), device_id_type=MESH)

    def remote(src, dst, send, recv, axis, shift):
        return pltpu.make_async_remote_copy(
            src_ref=src, dst_ref=dst, send_sem=send, recv_sem=recv, device_id=peer(axis, shift), device_id_type=MESH
        )

    barrier = pltpu.get_barrier_semaphore()
    greet(barrier, near)

    loads = [
        pltpu.make_async_copy(src, dst, load_sem.at[k])
        for k, (src, dst) in enumerate(
            ((v_hbm, vx), (diff_hbm, diff), (c_hbm.at[0], cx), (dec_hbm, dec), (c_hbm.at[2], cz), (c_hbm.at[1], cy), (offset_hbm, offset))
        )
    ]
    for copy in loads:
        copy.start()

    vx2, cy2, cz2, czz2 = (ref.reshape(1024, 128) for ref in (vx, cy, cz, czz))
    work1_2, work2_2, out2 = (ref.reshape(1024, 128) for ref in (work1, work2, out))

    def into_z(src2, dst2, blocks):
        for b in blocks:
            dst2[pl.ds(b, 128, stride=8), :] = src2[pl.ds(128 * b, 128), :].T

    for copy in loads[:4]:
        copy.wait()
    scale = [diff[a] * float(c * c) for a, c in enumerate((32, 32, 128))]
    half = [WEIGHT * s for s in scale]

    lane = lax.broadcasted_iota(jnp.int32, (128, 128), 1)
    blocks = [pl.ds(128 * b, 128) for b in range(8)]
    packed = jnp.zeros((128, 128), F32)
    for b, at in enumerate(blocks):
        packed = jnp.where(lane // 2 == b, pltpu.roll(vx2[at, :], 2 * b + 1, 1), packed)
    loads[4].wait()
    for b, at in enumerate(blocks):
        packed = jnp.where(lane == 16 + b, pltpu.roll(cz2[at, :], 17 + b, 1), packed)
    edge_rows[...] = packed.T
    edge[0] = edge_rows[pl.ds(1, 8, stride=2), :]
    edge[1] = edge_rows[pl.ds(0, 8, stride=2), :]
    edge[2] = edge_rows[pl.ds(16, 8), :]

    pl.semaphore_wait(barrier, len(near))
    greet(known.at[0], near)
    halos = [
        remote(edge.at[0], halo_z.at[0], halo_send.at[4], halo_recv.at[4], 2, -1),
        remote(edge.at[1], halo_z.at[1], halo_send.at[5], halo_recv.at[5], 2, 1),
        remote(edge.at[2], halo_z.at[2], halo_send.at[6], halo_recv.at[6], 2, 1),
        remote(v_hbm.at[:, 0, 0, :], halo_y.at[0], halo_send.at[1], halo_recv.at[1], 1, -1),
        remote(v_hbm.at[:, 3, 7, :], halo_y.at[1], halo_send.at[2], halo_recv.at[2], 1, 1),
        remote(c_hbm.at[1, :, 3, 7, :], halo_y.at[2], halo_send.at[3], halo_recv.at[3], 1, 1),
        remote(v_hbm.at[0], halo_x, halo_send.at[0], halo_recv.at[0], 0, -1),
    ]
    for copy in halos:
        copy.start()

    def excess_x(i):
        v = vx[i]
        return 1.0 + WEIGHT * (dec[i] * (1.0 + 3.0 * (v * v)))

    def matrix_row_x(i, carry):
        kx, lx, sx = carry
        rx[i], ax[i], bx[i], lx, kx, sx = eliminate(excess_x(i) + lx, kx, sx, half[0] * cx[i])
        return kx, lx, sx

    zero = jnp.zeros((4, 8, 128), F32)
    kx, lx, sx = rows_loop(1, 31, 1, matrix_row_x, (half[0] * cx[0], zero, excess_x(0)), 32)
    mx_own[0], mx_own[1], mx_own[2] = kx, sx, lx

    def send_matrix(axis, own, into, first, reach=(1, 2, 3, 4)):
        copies = []
        for j in far_first(sizes[axis]):
            if min(j, sizes[axis] - j) not in reach:
                continue
            k = first + j - 1
            copies.append(remote(own, into.at[j - 1], mat_send.at[k], mat_recv.at[k], axis, -j))
            copies[-1].start()
        return copies

    mats_x = send_matrix(0, mx_own, mx_in, 0, (1,))
    pl.semaphore_wait(known.at[0], len(near))
    greet(known.at[1], near_z)
    mats_x += send_matrix(0, mx_own, mx_in, 0, (2,))

    for copy in loads[5:]:
        copy.wait()

    def to_y(y, _):
        for xc in range(4):
            at = pl.ds(xc * 256 + y, 8, stride=32)
            vy[xc, y] = vx2[at, :]
            cyy[xc, y] = cy2[at, :]
        return 0

    rows_loop(0, 32, 1, to_y, 0, 32)

    def matrix_row_y(i, carry):
        ky, ly, sy = carry
        ry[:, i], ay[:, i], by[:, i], ly, ky, sy = eliminate(1.0 + ly, ky, sy, half[1] * cyy[:, i])
        return ky, ly, sy

    ky, ly, sy = rows_loop(1, 31, 1, matrix_row_y, (half[1] * cyy[:, 0], zero, zero + 1.0), 32)
    my_own[0], my_own[1], my_own[2] = ky, sy, ly
    first_y = sizes[0] - 1
    first_z = first_y + sizes[1] - 1
    mats_y = send_matrix(1, my_own, my_in, first_y)

    def at_y(y):
        return [pl.ds(xc * 256 + y, 8, stride=32) for xc in range(4)]

    def flux_y(y, carry):
        v, below = carry
        after = vy[:, y + 1]
        flux = scale[1] * (cyy[:, y] * (after - v))
        for xc, at in enumerate(at_y(y)):
            work1_2[at, :] = (flux - below)[xc]
        return after, flux

    v_last, below = rows_loop(0, 31, 1, flux_y, (vy[:, 0], zero), 32)
    for xc, at in enumerate(at_y(31)):
        work1_2[at, :] = -below[xc]
    for at in blocks:
        v = vx2[at, :]
        flux = jnp.where(lane < 127, scale[2] * (cz2[at, :] * (pltpu.roll(v, 127, 1) - v)), 0.0)
        work1_2[at, :] = work1_2[at, :] + (flux - pltpu.roll(flux, 1, 1))

    for copy in halos:
        copy.wait()

    hy = halo_y.reshape(3, 4, 8, 128)
    low = scale[1] * (hy[2] * (vy[:, 0] - hy[1]))
    high = scale[1] * (cyy[:, 31] * (hy[0] - v_last))
    for xc in range(4):
        at0, at31 = at_y(0)[xc], at_y(31)[xc]
        work1_2[at0, :] = work1_2[at0, :] - low[xc]
        work1_2[at31, :] = work1_2[at31, :] + high[xc]
    edge_fix[pl.ds(0, 8, stride=2), :] = scale[2] * (edge[2] * (halo_z[0] - edge[1]))
    edge_fix[pl.ds(1, 8, stride=2), :] = scale[2] * (halo_z[2] * (halo_z[1] - edge[0]))
    fix = jnp.concatenate([edge_fix[...], jnp.zeros((112, 128), F32)], axis=0).T
    outer = (lane == 0) | (lane == 127)
    for b, at in enumerate(blocks):
        work1_2[at, :] = work1_2[at, :] + jnp.where(outer, pltpu.roll(fix, 127 - 2 * b, 1), 0.0)

    z = lax.broadcasted_iota(jnp.int32, (1, 8, 128), 2)
    length = 128 * sizes[2]
    phase = lax.rem(z + (me[2] * 128 + offset[0]), length).astype(F32) * (2.0 * math.pi / length)
    forcing = 2.0 * jnp.sin(phase)

    def exchange(axis, own, into, first):
        copies = []
        for j in far_first(sizes[axis]):
            k = first + j - 1
            copies.append(remote(own, into.at[j - 1], rhs_send.at[k], rhs_recv.at[k], axis, -j))
            copies[-1].start()
        return copies

    def factors(axis, own, into, weights, copies):
        for copy in copies:
            copy.wait_recv()
        nodes = [tuple(own[k] for k in range(3))] + [tuple(into[j, k] for k in range(3)) for j in range(sizes[axis] - 1)]
        for k, value in enumerate(ring_factors(nodes)):
            weights[k] = value

    def solve(axis, own, into, weight, copies):
        for copy in copies:
            copy.wait_recv()
        pairs = [(own[0], own[1])] + [(into[j, 0], into[j, 1]) for j in range(sizes[axis] - 1)]
        return ring_apply(weight, pairs)

    halves = [slice(2 * c, 2 * c + 2) for c in range(2)]
    sent_x = []
    for c, at in enumerate(halves):

        def right_x(i, v, after, below):
            flux = scale[0] * (cx[i, at] * (after - v))
            right = (flux - below) + work1[i, at] - dec[i, at] * v * (1.0 + v * v) + forcing
            return right, flux

        def forward_x(i, carry):
            v, below, y, load = carry
            after = vx[i + 1, at]
            right, flux = right_x(i, v, after, below)
            y = right + ax[i - 1, at] * y
            work3[i, at] = y
            return after, flux, y, load + bx[i, at] * y

        v0, v1, v2 = vx[0, at], vx[1, at], vx[2, at]
        load, flux = right_x(0, v0, v1, 0.0)
        y, flux = right_x(1, v1, v2, flux)
        work3[1, at] = y
        v, below, y, load = rows_loop(2, 29, 1, forward_x, (v2, flux, y, load + bx[1, at] * y), 32)
        right, flux = right_x(31, v, halo_x[at], below)
        y = right + ax[30, at] * y
        work3[31, at] = y
        fx_own[c, 0] = load + bx[31, at] * y
        fx_own[c, 1] = ax[31, at] * y - flux
        sent_x.append(exchange(0, fx_own.at[c], fx_in.at[c], c * (sizes[0] - 1)))

    pl.semaphore_wait(known.at[1], len(near_z))
    greet(known.at[2], near_z)
    into_z(cz2, czz2, range(8))

    def matrix_row_z(i, carry):
        kz, lz, sz = carry
        rz[:, i], az[:, i], bz[:, i], lz, kz, sz = eliminate(1.0 + lz, kz, sz, half[2] * czz[:, i])
        return kz, lz, sz

    kz, lz, sz = rows_loop(1, 31, 1, matrix_row_z, (half[2] * czz[:, 0], zero, zero + 1.0), 32)
    coupling, left, excess = kz[0], sz[0], sz[1] + lz[0]
    for s in range(1, 4):
        inverse, alpha, beta, carried, coupling, left = eliminate(excess, coupling, left, kz[s])
        segz[0, s], segz[1, s], segz[2, s] = inverse, alpha, beta
        excess = carried + lz[s] + (sz[s + 1] if s < 3 else 0.0)
    mz_own[0], mz_own[1], mz_own[2] = coupling, left, excess

    pl.semaphore_wait(known.at[2], len(near_z))
    mats_z = send_matrix(2, mz_own, mz_in, first_z)
    factors(0, mx_own, mx_in, wx, mats_x)

    for c, at in enumerate(halves):
        node, after = solve(0, fx_own.at[c], fx_in.at[c], lambda k: wx[k, at], sent_x[c])

        def backward_x(i, u):
            u = (rx[i, at] * work3[i, at] + bx[i, at] * node) + ax[i, at] * u
            work1[i, at] = u
            return u

        rows_loop(31, 31, -1, backward_x, after, 32)
        work1[0, at] = node

    sent_y, first = [], 2 * (sizes[0] - 1)
    for c, at in enumerate(halves):

        def right_y(y):
            return jnp.stack([work1_2[pl.ds(xc * 256 + y, 8, stride=32), :] for xc in (2 * c, 2 * c + 1)])

        def forward_y(i, carry):
            y, load = carry
            y = right_y(i) + ay[at, i - 1] * y
            work2[at, i] = y
            return y, load + by[at, i] * y

        y = right_y(1)
        work2[at, 1] = y
        y, load = rows_loop(2, 30, 1, forward_y, (y, right_y(0) + by[at, 1] * y), 32)
        fy_own[c, 0] = load
        fy_own[c, 1] = ay[at, 31] * y
        sent_y.append(exchange(1, fy_own.at[c], fy_in.at[c], first))
        first += sizes[1] - 1

    factors(1, my_own, my_in, wy, mats_y)
    factors(2, mz_own, mz_in, wz, mats_z)

    zwork = work3.reshape(4, 32, 8, 128)
    zwork2 = work3.reshape(1024, 128)
    for c, at in enumerate(halves):
        node, after = solve(1, fy_own.at[c], fy_in.at[c], lambda k: wy[k, at], sent_y[c])

        def store_half(y, value):
            for m in range(2):
                work1_2[pl.ds((2 * c + m) * 256 + y, 8, stride=32), :] = value[m]

        def backward_y(i, u):
            u = (ry[at, i] * work2[at, i] + by[at, i] * node) + ay[at, i] * u
            store_half(i, u)
            return u

        rows_loop(31, 31, -1, backward_y, after, 32)
        store_half(0, node)
        into_z(work1_2, zwork2, range(4 * c, 4 * c + 4))

    def forward_z(i, carry):
        y, load = carry
        y = zwork[:, i] + az[:, i - 1] * y
        work2[:, i] = y
        return y, load + bz[:, i] * y

    y = zwork[:, 1]
    work2[:, 1] = y
    y, load = rows_loop(2, 30, 1, forward_z, (y, zwork[:, 0] + bz[:, 1] * y), 32)
    carried = az[:, 31] * y
    ys, left = [None], load[0]
    for s in range(1, 4):
        y = load[s] + carried[s - 1]
        if s > 1:
            y = y + segz[1, s - 1] * ys[-1]
        ys.append(y)
        left = left + segz[2, s] * y
    fz_own[0] = left
    fz_own[1] = carried[3] + segz[1, 3] * ys[3]

    sent_z = exchange(2, fz_own, fz_in, first)
    node, after = solve(2, fz_own, fz_in, lambda k: wz[k], sent_z)
    ends_z = [after]
    for s in (3, 2, 1):
        ends_z.insert(0, (segz[0, s] * ys[s] + segz[2, s] * node) + segz[1, s] * ends_z[0])
    starts_z = jnp.stack([node] + ends_z[:3])

    def backward_z(i, u):
        u = (rz[:, i] * work2[:, i] + bz[:, i] * starts_z) + az[:, i] * u
        zwork[:, i] = u
        return u

    rows_loop(31, 31, -1, backward_z, jnp.stack(ends_z), 32)
    zwork[:, 0] = starts_z

    for b in range(8):
        at = pl.ds(128 * b, 128)
        out2[at, :] = vx2[at, :] + zwork2[pl.ds(b, 128, stride=8), :].T
    for copy in mats_x + mats_y + mats_z + sum(sent_x, []) + sum(sent_y, []) + sent_z:
        copy.wait_send()


def on_device(sizes, density, conductance, decay_rate, diffusion_numbers, plane_offset):
    nx, ny, nz = sizes
    grid = (32, 4, 8, 128)
    lines = (4, 32, 8, 128)
    one = (4, 8, 128)
    two = (2, 8, 128)
    peers = nx + ny + nz - 3
    vmem = lambda *shape: pltpu.VMEM(shape, F32)
    dma = lambda n: pltpu.SemaphoreType.DMA((n,))
    operands = (
        diffusion_numbers,
        plane_offset,
        density.reshape(grid),
        conductance.reshape((3,) + grid),
        decay_rate.reshape(grid),
    )
    updated = pl.pallas_call(
        functools.partial(kernel, sizes),
        out_shape=jax.ShapeDtypeStruct(grid, F32),
        in_specs=[pl.BlockSpec(memory_space=pl.ANY)] * len(operands),
        out_specs=pl.BlockSpec(memory_space=pltpu.VMEM),
        scratch_shapes=[pltpu.SMEM((3,), F32), pltpu.SMEM((1,), jnp.int32)]
        + [vmem(*grid)] * 5
        + [vmem(*lines)] * 3
        + [vmem(*grid)] * 3
        + [vmem(*lines)] * 6
        + [vmem(3, 4, 8, 128)]
        + [vmem(2 * nx - 1, *one), vmem(2 * ny - 1, *one), vmem(2 * nz - 1, 8, 128)]
        + [vmem(*grid), vmem(*lines), vmem(*grid)]
        + [vmem(*one), vmem(3, 32, 128), vmem(3, 8, 128), vmem(3, 8, 128), vmem(128, 128), vmem(16, 128)]
        + [vmem(3, *one), vmem(3, *one), vmem(3, 8, 128)]
        + [vmem(nx - 1, 3, *one), vmem(ny - 1, 3, *one), vmem(nz - 1, 3, 8, 128)]
        + [vmem(2, 2, *two), vmem(2, 2, *two), vmem(2, 8, 128)]
        + [vmem(2, nx - 1, 2, *two), vmem(2, ny - 1, 2, *two), vmem(nz - 1, 2, 8, 128)]
        + [dma(7), dma(7), dma(7), dma(peers), dma(peers), dma(2 * peers), dma(2 * peers), pltpu.SemaphoreType.REGULAR((3,))],
        compiler_params=pltpu.CompilerParams(collective_id=0, has_side_effects=True, vmem_limit_bytes=40 * 1024 * 1024),
        name="adi_step",
    )(*(x if x.size == 1 else pltpu.with_memory_space_constraint(x, pltpu.MemorySpace.HBM) for x in operands))
    return updated.reshape(density.shape)


def solution(mesh):
    sizes = tuple(mesh.shape[a] for a in AXES)
    placed = (P("gx", "gy", "gz"), P(None, "gx", "gy", "gz"), P("gx", "gy", "gz"), P(), P())
    return jax.shard_map(
        functools.partial(on_device, sizes), mesh=mesh, in_specs=placed, out_specs=P("gx", "gy", "gz"), check_vma=False
    )
```

```python
import functools
import math

import jax
import jax.numpy as jnp
from jax import lax
from jax.experimental import pallas as pl
from jax.experimental.pallas import tpu as pltpu
from jax.sharding import PartitionSpec as P

MESH = pl.DeviceIdType.MESH
F32 = jnp.float32
AXES = ("gx", "gy", "gz")
WEIGHT = 0.5


def far_first(n):
    return sorted(range(1, n), key=lambda j: (-min(j, n - j), j))


def rows_loop(lo, count, step, body, carry, unroll):
    if unroll >= count:
        for m in range(count):
            carry = body(lo + step * m, carry)
        return carry
    whole = count // unroll

    def block(k, c):
        for m in range(unroll):
            c = body(lo + step * (k * unroll + m), c)
        return c

    carry = lax.fori_loop(0, whole, block, carry)
    for m in range(whole * unroll, count):
        carry = body(lo + step * m, carry)
    return carry


def eliminate(excess, coupling, left, e):
    inverse = 1.0 / (excess + coupling + e)
    alpha, beta, leak = e * inverse, coupling * inverse, excess * inverse
    return inverse, alpha, beta, e * leak, e * beta, left + coupling * leak


def ring_factors(nodes):
    n = len(nodes)
    total = [nodes[j][1] + nodes[j - 1][2] for j in range(n)]
    alphas, betas = {}, {}
    coupling, excess, leak1 = nodes[1][0], total[2], total[1]
    for j in range(2, n):
        _, alphas[j], betas[j], carried, coupling, leak1 = eliminate(excess, coupling, leak1, nodes[j][0])
        excess = carried + total[(j + 1) % n]
    leak0 = excess
    c = nodes[0][0] + coupling
    inverse = 1.0 / (leak0 * leak1 + c * (leak0 + leak1))
    to0, to1 = {}, {}
    p, q = jnp.zeros_like(c), jnp.ones_like(c)
    for j in reversed(range(2, n)):
        p, q = betas[j] + alphas[j] * p, alphas[j] * q
        to1[j], to0[j] = p, q
    return [to0[j] for j in range(2, n)] + [to1[j] for j in range(2, n)] + [(leak1 + c) * inverse, c * inverse, (leak0 + c) * inverse]


def ring_apply(factors, loads):
    n = len(loads)
    right = [loads[j][0] + loads[j - 1][1] for j in range(n)]
    sum0, sum1 = right[0], right[1]
    for j in range(2, n):
        sum0 = sum0 + factors(j - 2) * right[j]
        sum1 = sum1 + factors(n - 2 + j - 2) * right[j]
    g00, g01, g11 = (factors(2 * (n - 2) + k) for k in range(3))
    return g00 * sum0 + g01 * sum1, g01 * sum0 + g11 * sum1


def kernel(
    sizes,
    diff_hbm, offset_hbm, v_hbm, c_hbm, dec_hbm, out,
    diff, offset, vx, cx, cy, cz, dec, vy, cyy, czz,
    ax, bx, rx, ay, by, ry, az, bz, rz, segz,
    wx, wy, wz, work1, work2, work3,
    halo_x, halo_y, halo_z, edge, edge_rows, edge_fix,
    mx_own, my_own, mz_own, mx_in, my_in, mz_in,
    fx_own, fy_own, fz_own, fx_in, fy_in, fz_in,
    load_sem, halo_send, halo_recv, mat_send, mat_recv, rhs_send, rhs_recv, known,
):
    me = [lax.axis_index(a) for a in AXES]

    def peer(axis, shift):
        n = sizes[axis]
        return {AXES[axis]: lax.rem(me[axis] + (shift % n), n)}

    near = [(0, -1), (0, 1), (2, -1), (2, 1), (1, -1), (1, 1), (1, -2), (1, 2)]
    near_z = near[2:4]

    def greet(sem, peers):
        for axis, shift in peers:
            pl.semaphore_signal(sem, inc=1, device_id=peer(axis, shift), device_id_type=MESH)

    def remote(src, dst, send, recv, axis, shift):
        return pltpu.make_async_remote_copy(
            src_ref=src, dst_ref=dst, send_sem=send, recv_sem=recv, device_id=peer(axis, shift), device_id_type=MESH
        )

    barrier = pltpu.get_barrier_semaphore()
    greet(barrier, near)

    loads = [
        pltpu.make_async_copy(src, dst, load_sem.at[k])
        for k, (src, dst) in enumerate(
            ((v_hbm, vx), (diff_hbm, diff), (c_hbm.at[0], cx), (dec_hbm, dec), (c_hbm.at[2], cz), (c_hbm.at[1], cy), (offset_hbm, offset))
        )
    ]
    for copy in loads:
        copy.start()

    vx2, cy2, cz2, czz2 = (ref.reshape(1024, 128) for ref in (vx, cy, cz, czz))
    work1_2, work2_2, out2 = (ref.reshape(1024, 128) for ref in (work1, work2, out))

    def into_z(src2, dst2, blocks):
        for b in blocks:
            dst2[pl.ds(b, 128, stride=8), :] = src2[pl.ds(128 * b, 128), :].T

    for copy in loads[:4]:
        copy.wait()
    scale = [diff[a] * float(c * c) for a, c in enumerate((32, 32, 128))]
    half = [WEIGHT * s for s in scale]

    lane = lax.broadcasted_iota(jnp.int32, (128, 128), 1)
    blocks = [pl.ds(128 * b, 128) for b in range(8)]
    packed = jnp.zeros((128, 128), F32)
    for b, at in enumerate(blocks):
        packed = jnp.where(lane // 2 == b, pltpu.roll(vx2[at, :], 2 * b + 1, 1), packed)
    loads[4].wait()
    for b, at in enumerate(blocks):
        packed = jnp.where(lane == 16 + b, pltpu.roll(cz2[at, :], 17 + b, 1), packed)
    edge_rows[...] = packed.T
    edge[0] = edge_rows[pl.ds(1, 8, stride=2), :]
    edge[1] = edge_rows[pl.ds(0, 8, stride=2), :]
    edge[2] = edge_rows[pl.ds(16, 8), :]

    pl.semaphore_wait(barrier, len(near))
    greet(known.at[0], near)
    halos = [
        remote(vx.at[0], halo_x, halo_send.at[0], halo_recv.at[0], 0, -1),
        remote(edge.at[0], halo_z.at[0], halo_send.at[4], halo_recv.at[4], 2, -1),
        remote(edge.at[1], halo_z.at[1], halo_send.at[5], halo_recv.at[5], 2, 1),
        remote(edge.at[2], halo_z.at[2], halo_send.at[6], halo_recv.at[6], 2, 1),
        remote(vx.at[:, 0, 0, :], halo_y.at[0], halo_send.at[1], halo_recv.at[1], 1, -1),
        remote(vx.at[:, 3, 7, :], halo_y.at[1], halo_send.at[2], halo_recv.at[2], 1, 1),
        remote(c_hbm.at[1, :, 3, 7, :], halo_y.at[2], halo_send.at[3], halo_recv.at[3], 1, 1),
    ]
    for copy in halos:
        copy.start()

    def excess_x(i):
        v = vx[i]
        return 1.0 + WEIGHT * (dec[i] * (1.0 + 3.0 * (v * v)))

    def matrix_row_x(i, carry):
        kx, lx, sx = carry
        rx[i], ax[i], bx[i], lx, kx, sx = eliminate(excess_x(i) + lx, kx, sx, half[0] * cx[i])
        return kx, lx, sx

    zero = jnp.zeros((4, 8, 128), F32)
    kx, lx, sx = rows_loop(1, 31, 1, matrix_row_x, (half[0] * cx[0], zero, excess_x(0)), 32)
    mx_own[0], mx_own[1], mx_own[2] = kx, sx, lx

    def send_matrix(axis, own, into, first):
        copies = []
        for j in far_first(sizes[axis]):
            k = first + j - 1
            copies.append(remote(own, into.at[j - 1], mat_send.at[k], mat_recv.at[k], axis, -j))
            copies[-1].start()
        return copies

    pl.semaphore_wait(known.at[0], len(near))
    greet(known.at[1], near_z)
    mats_x = send_matrix(0, mx_own, mx_in, 0)

    for copy in loads[5:]:
        copy.wait()

    def to_y(y, _):
        for xc in range(4):
            at = pl.ds(xc * 256 + y, 8, stride=32)
            vy[xc, y] = vx2[at, :]
            cyy[xc, y] = cy2[at, :]
        return 0

    rows_loop(0, 32, 1, to_y, 0, 32)

    def matrix_row_y(i, carry):
        ky, ly, sy = carry
        ry[:, i], ay[:, i], by[:, i], ly, ky, sy = eliminate(1.0 + ly, ky, sy, half[1] * cyy[:, i])
        return ky, ly, sy

    ky, ly, sy = rows_loop(1, 31, 1, matrix_row_y, (half[1] * cyy[:, 0], zero, zero + 1.0), 32)
    my_own[0], my_own[1], my_own[2] = ky, sy, ly
    first_y = sizes[0] - 1
    first_z = first_y + sizes[1] - 1
    mats_y = send_matrix(1, my_own, my_in, first_y)

    def at_y(y):
        return [pl.ds(xc * 256 + y, 8, stride=32) for xc in range(4)]

    def flux_y(y, carry):
        v, below = carry
        after = vy[:, y + 1]
        flux = scale[1] * (cyy[:, y] * (after - v))
        for xc, at in enumerate(at_y(y)):
            work1_2[at, :] = (flux - below)[xc]
        return after, flux

    v_last, below = rows_loop(0, 31, 1, flux_y, (vy[:, 0], zero), 32)
    for xc, at in enumerate(at_y(31)):
        work1_2[at, :] = -below[xc]
    for at in blocks:
        v = vx2[at, :]
        flux = jnp.where(lane < 127, scale[2] * (cz2[at, :] * (pltpu.roll(v, 127, 1) - v)), 0.0)
        work1_2[at, :] = work1_2[at, :] + (flux - pltpu.roll(flux, 1, 1))

    for copy in halos:
        copy.wait()

    hy = halo_y.reshape(3, 4, 8, 128)
    low = scale[1] * (hy[2] * (vy[:, 0] - hy[1]))
    high = scale[1] * (cyy[:, 31] * (hy[0] - v_last))
    for xc in range(4):
        at0, at31 = at_y(0)[xc], at_y(31)[xc]
        work1_2[at0, :] = work1_2[at0, :] - low[xc]
        work1_2[at31, :] = work1_2[at31, :] + high[xc]
    edge_fix[pl.ds(0, 8, stride=2), :] = scale[2] * (edge[2] * (halo_z[0] - edge[1]))
    edge_fix[pl.ds(1, 8, stride=2), :] = scale[2] * (halo_z[2] * (halo_z[1] - edge[0]))
    fix = jnp.concatenate([edge_fix[...], jnp.zeros((112, 128), F32)], axis=0).T
    outer = (lane == 0) | (lane == 127)
    for b, at in enumerate(blocks):
        work1_2[at, :] = work1_2[at, :] + jnp.where(outer, pltpu.roll(fix, 127 - 2 * b, 1), 0.0)

    z = lax.broadcasted_iota(jnp.int32, (1, 8, 128), 2)
    length = 128 * sizes[2]
    phase = lax.rem(z + (me[2] * 128 + offset[0]), length).astype(F32) * (2.0 * math.pi / length)
    forcing = 2.0 * jnp.sin(phase)

    def exchange(axis, own, into, first):
        copies = []
        for j in far_first(sizes[axis]):
            k = first + j - 1
            copies.append(remote(own, into.at[j - 1], rhs_send.at[k], rhs_recv.at[k], axis, -j))
            copies[-1].start()
        return copies

    def factors(axis, own, into, weights, copies):
        for copy in copies:
            copy.wait_recv()
        nodes = [tuple(own[k] for k in range(3))] + [tuple(into[j, k] for k in range(3)) for j in range(sizes[axis] - 1)]
        for k, value in enumerate(ring_factors(nodes)):
            weights[k] = value

    def solve(axis, own, into, weight, copies):
        for copy in copies:
            copy.wait_recv()
        pairs = [(own[0], own[1])] + [(into[j, 0], into[j, 1]) for j in range(sizes[axis] - 1)]
        return ring_apply(weight, pairs)

    halves = [slice(2 * c, 2 * c + 2) for c in range(2)]
    sent_x = []
    for c, at in enumerate(halves):

        def right_x(i, v, after, below):
            flux = scale[0] * (cx[i, at] * (after - v))
            right = (flux - below) + work1[i, at] - dec[i, at] * v * (1.0 + v * v) + forcing
            return right, flux

        def forward_x(i, carry):
            v, below, y, load = carry
            after = vx[i + 1, at]
            right, flux = right_x(i, v, after, below)
            y = right + ax[i - 1, at] * y
            work3[i, at] = y
            return after, flux, y, load + bx[i, at] * y

        v0, v1, v2 = vx[0, at], vx[1, at], vx[2, at]
        load, flux = right_x(0, v0, v1, 0.0)
        y, flux = right_x(1, v1, v2, flux)
        work3[1, at] = y
        v, below, y, load = rows_loop(2, 29, 1, forward_x, (v2, flux, y, load + bx[1, at] * y), 32)
        right, flux = right_x(31, v, halo_x[at], below)
        y = right + ax[30, at] * y
        work3[31, at] = y
        fx_own[c, 0] = load + bx[31, at] * y
        fx_own[c, 1] = ax[31, at] * y - flux
        sent_x.append(exchange(0, fx_own.at[c], fx_in.at[c], c * (sizes[0] - 1)))

    pl.semaphore_wait(known.at[1], len(near_z))
    greet(known.at[2], near_z)
    into_z(cz2, czz2, range(8))

    def matrix_row_z(i, carry):
        kz, lz, sz = carry
        rz[:, i], az[:, i], bz[:, i], lz, kz, sz = eliminate(1.0 + lz, kz, sz, half[2] * czz[:, i])
        return kz, lz, sz

    kz, lz, sz = rows_loop(1, 31, 1, matrix_row_z, (half[2] * czz[:, 0], zero, zero + 1.0), 32)
    coupling, left, excess = kz[0], sz[0], sz[1] + lz[0]
    for s in range(1, 4):
        inverse, alpha, beta, carried, coupling, left = eliminate(excess, coupling, left, kz[s])
        segz[0, s], segz[1, s], segz[2, s] = inverse, alpha, beta
        excess = carried + lz[s] + (sz[s + 1] if s < 3 else 0.0)
    mz_own[0], mz_own[1], mz_own[2] = coupling, left, excess

    pl.semaphore_wait(known.at[2], len(near_z))
    mats_z = send_matrix(2, mz_own, mz_in, first_z)
    factors(0, mx_own, mx_in, wx, mats_x)

    for c, at in enumerate(halves):
        node, after = solve(0, fx_own.at[c], fx_in.at[c], lambda k: wx[k, at], sent_x[c])

        def backward_x(i, u):
            u = (rx[i, at] * work3[i, at] + bx[i, at] * node) + ax[i, at] * u
            work1[i, at] = u
            return u

        rows_loop(31, 31, -1, backward_x, after, 32)
        work1[0, at] = node

    sent_y, first = [], 2 * (sizes[0] - 1)
    for c, at in enumerate(halves):

        def right_y(y):
            return jnp.stack([work1_2[pl.ds(xc * 256 + y, 8, stride=32), :] for xc in (2 * c, 2 * c + 1)])

        def forward_y(i, carry):
            y, load = carry
            y = right_y(i) + ay[at, i - 1] * y
            work2[at, i] = y
            return y, load + by[at, i] * y

        y = right_y(1)
        work2[at, 1] = y
        y, load = rows_loop(2, 30, 1, forward_y, (y, right_y(0) + by[at, 1] * y), 32)
        fy_own[c, 0] = load
        fy_own[c, 1] = ay[at, 31] * y
        sent_y.append(exchange(1, fy_own.at[c], fy_in.at[c], first))
        first += sizes[1] - 1

    factors(1, my_own, my_in, wy, mats_y)
    factors(2, mz_own, mz_in, wz, mats_z)

    zwork = work3.reshape(4, 32, 8, 128)
    zwork2 = work3.reshape(1024, 128)
    for c, at in enumerate(halves):
        node, after = solve(1, fy_own.at[c], fy_in.at[c], lambda k: wy[k, at], sent_y[c])

        def store_half(y, value):
            for m in range(2):
                work1_2[pl.ds((2 * c + m) * 256 + y, 8, stride=32), :] = value[m]

        def backward_y(i, u):
            u = (ry[at, i] * work2[at, i] + by[at, i] * node) + ay[at, i] * u
            store_half(i, u)
            return u

        rows_loop(31, 31, -1, backward_y, after, 32)
        store_half(0, node)
        into_z(work1_2, zwork2, range(4 * c, 4 * c + 4))

    def forward_z(i, carry):
        y, load = carry
        y = zwork[:, i] + az[:, i - 1] * y
        work2[:, i] = y
        return y, load + bz[:, i] * y

    y = zwork[:, 1]
    work2[:, 1] = y
    y, load = rows_loop(2, 30, 1, forward_z, (y, zwork[:, 0] + bz[:, 1] * y), 32)
    carried = az[:, 31] * y
    ys, left = [None], load[0]
    for s in range(1, 4):
        y = load[s] + carried[s - 1]
        if s > 1:
            y = y + segz[1, s - 1] * ys[-1]
        ys.append(y)
        left = left + segz[2, s] * y
    fz_own[0] = left
    fz_own[1] = carried[3] + segz[1, 3] * ys[3]

    sent_z = exchange(2, fz_own, fz_in, first)
    node, after = solve(2, fz_own, fz_in, lambda k: wz[k], sent_z)
    ends_z = [after]
    for s in (3, 2, 1):
        ends_z.insert(0, (segz[0, s] * ys[s] + segz[2, s] * node) + segz[1, s] * ends_z[0])
    starts_z = jnp.stack([node] + ends_z[:3])

    def backward_z(i, u):
        u = (rz[:, i] * work2[:, i] + bz[:, i] * starts_z) + az[:, i] * u
        zwork[:, i] = u
        return u

    rows_loop(31, 31, -1, backward_z, jnp.stack(ends_z), 32)
    zwork[:, 0] = starts_z

    for b in range(8):
        at = pl.ds(128 * b, 128)
        out2[at, :] = vx2[at, :] + zwork2[pl.ds(b, 128, stride=8), :].T
    for copy in mats_x + mats_y + mats_z + sum(sent_x, []) + sum(sent_y, []) + sent_z:
        copy.wait_send()


def on_device(sizes, density, conductance, decay_rate, diffusion_numbers, plane_offset):
    nx, ny, nz = sizes
    grid = (32, 4, 8, 128)
    lines = (4, 32, 8, 128)
    one = (4, 8, 128)
    two = (2, 8, 128)
    peers = nx + ny + nz - 3
    vmem = lambda *shape: pltpu.VMEM(shape, F32)
    dma = lambda n: pltpu.SemaphoreType.DMA((n,))
    operands = (
        diffusion_numbers,
        plane_offset,
        density.reshape(grid),
        conductance.reshape((3,) + grid),
        decay_rate.reshape(grid),
    )
    updated = pl.pallas_call(
        functools.partial(kernel, sizes),
        out_shape=jax.ShapeDtypeStruct(grid, F32),
        in_specs=[pl.BlockSpec(memory_space=pl.ANY)] * len(operands),
        out_specs=pl.BlockSpec(memory_space=pltpu.VMEM),
        scratch_shapes=[pltpu.SMEM((3,), F32), pltpu.SMEM((1,), jnp.int32)]
        + [vmem(*grid)] * 5
        + [vmem(*lines)] * 3
        + [vmem(*grid)] * 3
        + [vmem(*lines)] * 6
        + [vmem(3, 4, 8, 128)]
        + [vmem(2 * nx - 1, *one), vmem(2 * ny - 1, *one), vmem(2 * nz - 1, 8, 128)]
        + [vmem(*grid), vmem(*lines), vmem(*grid)]
        + [vmem(*one), vmem(3, 32, 128), vmem(3, 8, 128), vmem(3, 8, 128), vmem(128, 128), vmem(16, 128)]
        + [vmem(3, *one), vmem(3, *one), vmem(3, 8, 128)]
        + [vmem(nx - 1, 3, *one), vmem(ny - 1, 3, *one), vmem(nz - 1, 3, 8, 128)]
        + [vmem(2, 2, *two), vmem(2, 2, *two), vmem(2, 8, 128)]
        + [vmem(2, nx - 1, 2, *two), vmem(2, ny - 1, 2, *two), vmem(nz - 1, 2, 8, 128)]
        + [dma(7), dma(7), dma(7), dma(peers), dma(peers), dma(2 * peers), dma(2 * peers), pltpu.SemaphoreType.REGULAR((3,))],
        compiler_params=pltpu.CompilerParams(collective_id=0, has_side_effects=True, vmem_limit_bytes=40 * 1024 * 1024),
        name="adi_step",
    )(*(x if x.size == 1 else pltpu.with_memory_space_constraint(x, pltpu.MemorySpace.HBM) for x in operands))
    return updated.reshape(density.shape)


def solution(mesh):
    sizes = tuple(mesh.shape[a] for a in AXES)
    placed = (P("gx", "gy", "gz"), P(None, "gx", "gy", "gz"), P("gx", "gy", "gz"), P(), P())
    return jax.shard_map(
        functools.partial(on_device, sizes), mesh=mesh, in_specs=placed, out_specs=P("gx", "gy", "gz"), check_vma=False
    )
```

```python
import functools
import math

import jax
import jax.numpy as jnp
from jax import lax
from jax.experimental import pallas as pl
from jax.experimental.pallas import tpu as pltpu
from jax.sharding import PartitionSpec as P

MESH = pl.DeviceIdType.MESH
F32 = jnp.float32
AXES = ("gx", "gy", "gz")
WEIGHT = 0.5


def far_first(n):
    return sorted(range(1, n), key=lambda j: (-min(j, n - j), j))


def rows_loop(lo, count, step, body, carry, unroll):
    if unroll >= count:
        for m in range(count):
            carry = body(lo + step * m, carry)
        return carry
    whole = count // unroll

    def block(k, c):
        for m in range(unroll):
            c = body(lo + step * (k * unroll + m), c)
        return c

    carry = lax.fori_loop(0, whole, block, carry)
    for m in range(whole * unroll, count):
        carry = body(lo + step * m, carry)
    return carry


def eliminate(excess, coupling, left, e):
    inverse = 1.0 / (excess + coupling + e)
    alpha, beta, leak = e * inverse, coupling * inverse, excess * inverse
    return inverse, alpha, beta, e * leak, e * beta, left + coupling * leak


def ring_factors(nodes):
    n = len(nodes)
    total = [nodes[j][1] + nodes[j - 1][2] for j in range(n)]
    alphas, betas = {}, {}
    coupling, excess, leak1 = nodes[1][0], total[2], total[1]
    for j in range(2, n):
        _, alphas[j], betas[j], carried, coupling, leak1 = eliminate(excess, coupling, leak1, nodes[j][0])
        excess = carried + total[(j + 1) % n]
    leak0 = excess
    c = nodes[0][0] + coupling
    inverse = 1.0 / (leak0 * leak1 + c * (leak0 + leak1))
    to0, to1 = {}, {}
    p, q = jnp.zeros_like(c), jnp.ones_like(c)
    for j in reversed(range(2, n)):
        p, q = betas[j] + alphas[j] * p, alphas[j] * q
        to1[j], to0[j] = p, q
    return [to0[j] for j in range(2, n)] + [to1[j] for j in range(2, n)] + [(leak1 + c) * inverse, c * inverse, (leak0 + c) * inverse]


def ring_apply(factors, loads):
    n = len(loads)
    right = [loads[j][0] + loads[j - 1][1] for j in range(n)]
    sum0, sum1 = right[0], right[1]
    for j in range(2, n):
        sum0 = sum0 + factors(j - 2) * right[j]
        sum1 = sum1 + factors(n - 2 + j - 2) * right[j]
    g00, g01, g11 = (factors(2 * (n - 2) + k) for k in range(3))
    return g00 * sum0 + g01 * sum1, g01 * sum0 + g11 * sum1


def kernel(
    sizes,
    diff_hbm, offset_hbm, v_hbm, c_hbm, dec_hbm, out,
    diff, offset, vx, cx, cy, cz, dec, vy, cyy, czz,
    ax, bx, rx, ay, by, ry, az, bz, rz, segz,
    wx, wy, wz, work1, work2, work3,
    halo_x, halo_y, halo_z, edge, edge_rows, edge_fix,
    mx_own, my_own, mz_own, mx_in, my_in, mz_in,
    fx_own, fy_own, fz_own, fx_in, fy_in, fz_in,
    load_sem, halo_send, halo_recv, mat_send, mat_recv, rhs_send, rhs_recv, known,
):
    me = [lax.axis_index(a) for a in AXES]

    def peer(axis, shift):
        n = sizes[axis]
        return {AXES[axis]: lax.rem(me[axis] + (shift % n), n)}

    near = [(0, -1), (0, 1), (2, -1), (2, 1), (1, -1), (1, 1), (1, -2), (1, 2)]
    near_z = near[2:4]

    def greet(sem, peers):
        for axis, shift in peers:
            pl.semaphore_signal(sem, inc=1, device_id=peer(axis, shift), device_id_type=MESH)

    def remote(src, dst, send, recv, axis, shift):
        return pltpu.make_async_remote_copy(
            src_ref=src, dst_ref=dst, send_sem=send, recv_sem=recv, device_id=peer(axis, shift), device_id_type=MESH
        )

    barrier = pltpu.get_barrier_semaphore()
    greet(barrier, near)

    loads = [
        pltpu.make_async_copy(src, dst, load_sem.at[k])
        for k, (src, dst) in enumerate(
            ((v_hbm, vx), (diff_hbm, diff), (c_hbm.at[0], cx), (dec_hbm, dec), (c_hbm.at[2], cz), (c_hbm.at[1], cy), (offset_hbm, offset))
        )
    ]
    for copy in loads:
        copy.start()

    vx2, cy2, cz2, czz2 = (ref.reshape(1024, 128) for ref in (vx, cy, cz, czz))
    work1_2, work2_2, out2 = (ref.reshape(1024, 128) for ref in (work1, work2, out))

    def into_z(src2, dst2, blocks):
        for b in blocks:
            dst2[pl.ds(b, 128, stride=8), :] = src2[pl.ds(128 * b, 128), :].T

    for copy in loads[:4]:
        copy.wait()
    scale = [diff[a] * float(c * c) for a, c in enumerate((32, 32, 128))]
    half = [WEIGHT * s for s in scale]

    lane = lax.broadcasted_iota(jnp.int32, (128, 128), 1)
    blocks = [pl.ds(128 * b, 128) for b in range(8)]
    packed = jnp.zeros((128, 128), F32)
    for b, at in enumerate(blocks):
        packed = jnp.where(lane // 2 == b, pltpu.roll(vx2[at, :], 2 * b + 1, 1), packed)
    loads[4].wait()
    for b, at in enumerate(blocks):
        packed = jnp.where(lane == 16 + b, pltpu.roll(cz2[at, :], 17 + b, 1), packed)
    edge_rows[...] = packed.T
    edge[0] = edge_rows[pl.ds(1, 8, stride=2), :]
    edge[1] = edge_rows[pl.ds(0, 8, stride=2), :]
    edge[2] = edge_rows[pl.ds(16, 8), :]

    pl.semaphore_wait(barrier, len(near))
    greet(known.at[0], near)
    halos = [
        remote(vx.at[0], halo_x, halo_send.at[0], halo_recv.at[0], 0, -1),
        remote(edge.at[0], halo_z.at[0], halo_send.at[4], halo_recv.at[4], 2, -1),
        remote(edge.at[1], halo_z.at[1], halo_send.at[5], halo_recv.at[5], 2, 1),
        remote(edge.at[2], halo_z.at[2], halo_send.at[6], halo_recv.at[6], 2, 1),
        remote(vx.at[:, 0, 0, :], halo_y.at[0], halo_send.at[1], halo_recv.at[1], 1, -1),
        remote(vx.at[:, 3, 7, :], halo_y.at[1], halo_send.at[2], halo_recv.at[2], 1, 1),
        remote(c_hbm.at[1, :, 3, 7, :], halo_y.at[2], halo_send.at[3], halo_recv.at[3], 1, 1),
    ]
    for copy in halos:
        copy.start()

    def excess_x(i):
        v = vx[i]
        return 1.0 + WEIGHT * (dec[i] * (1.0 + 3.0 * (v * v)))

    def matrix_row_x(i, carry):
        kx, lx, sx = carry
        rx[i], ax[i], bx[i], lx, kx, sx = eliminate(excess_x(i) + lx, kx, sx, half[0] * cx[i])
        return kx, lx, sx

    zero = jnp.zeros((4, 8, 128), F32)
    kx, lx, sx = rows_loop(1, 31, 1, matrix_row_x, (half[0] * cx[0], zero, excess_x(0)), 32)
    mx_own[0], mx_own[1], mx_own[2] = kx, sx, lx

    def send_matrix(axis, own, into, first):
        copies = []
        for j in far_first(sizes[axis]):
            k = first + j - 1
            copies.append(remote(own, into.at[j - 1], mat_send.at[k], mat_recv.at[k], axis, -j))
            copies[-1].start()
        return copies

    pl.semaphore_wait(known.at[0], len(near))
    greet(known.at[1], near_z)
    mats_x = send_matrix(0, mx_own, mx_in, 0)

    for copy in loads[5:]:
        copy.wait()

    def to_y(y, _):
        for xc in range(4):
            at = pl.ds(xc * 256 + y, 8, stride=32)
            vy[xc, y] = vx2[at, :]
            cyy[xc, y] = cy2[at, :]
        return 0

    rows_loop(0, 32, 1, to_y, 0, 32)

    first_y = sizes[0] - 1
    first_z = first_y + sizes[1] - 1

    def at_y(y):
        return [pl.ds(xc * 256 + y, 8, stride=32) for xc in range(4)]

    def flux_y(y, carry):
        v, below = carry
        after = vy[:, y + 1]
        flux = scale[1] * (cyy[:, y] * (after - v))
        for xc, at in enumerate(at_y(y)):
            work1_2[at, :] = (flux - below)[xc]
        return after, flux

    v_last, below = rows_loop(0, 31, 1, flux_y, (vy[:, 0], zero), 32)
    for xc, at in enumerate(at_y(31)):
        work1_2[at, :] = -below[xc]
    for at in blocks:
        v = vx2[at, :]
        flux = jnp.where(lane < 127, scale[2] * (cz2[at, :] * (pltpu.roll(v, 127, 1) - v)), 0.0)
        work1_2[at, :] = work1_2[at, :] + (flux - pltpu.roll(flux, 1, 1))

    def matrix_row_y(i, carry):
        ky, ly, sy = carry
        ry[:, i], ay[:, i], by[:, i], ly, ky, sy = eliminate(1.0 + ly, ky, sy, half[1] * cyy[:, i])
        return ky, ly, sy

    ky, ly, sy = rows_loop(1, 31, 1, matrix_row_y, (half[1] * cyy[:, 0], zero, zero + 1.0), 32)
    my_own[0], my_own[1], my_own[2] = ky, sy, ly
    mats_y = send_matrix(1, my_own, my_in, first_y)

    for copy in halos:
        copy.wait()

    hy = halo_y.reshape(3, 4, 8, 128)
    low = scale[1] * (hy[2] * (vy[:, 0] - hy[1]))
    high = scale[1] * (cyy[:, 31] * (hy[0] - v_last))
    for xc in range(4):
        at0, at31 = at_y(0)[xc], at_y(31)[xc]
        work1_2[at0, :] = work1_2[at0, :] - low[xc]
        work1_2[at31, :] = work1_2[at31, :] + high[xc]
    edge_fix[pl.ds(0, 8, stride=2), :] = scale[2] * (edge[2] * (halo_z[0] - edge[1]))
    edge_fix[pl.ds(1, 8, stride=2), :] = scale[2] * (halo_z[2] * (halo_z[1] - edge[0]))
    fix = jnp.concatenate([edge_fix[...], jnp.zeros((112, 128), F32)], axis=0).T
    outer = (lane == 0) | (lane == 127)
    for b, at in enumerate(blocks):
        work1_2[at, :] = work1_2[at, :] + jnp.where(outer, pltpu.roll(fix, 127 - 2 * b, 1), 0.0)

    z = lax.broadcasted_iota(jnp.int32, (1, 8, 128), 2)
    length = 128 * sizes[2]
    phase = lax.rem(z + (me[2] * 128 + offset[0]), length).astype(F32) * (2.0 * math.pi / length)
    forcing = 2.0 * jnp.sin(phase)

    def exchange(axis, own, into, first):
        copies = []
        for j in far_first(sizes[axis]):
            k = first + j - 1
            copies.append(remote(own, into.at[j - 1], rhs_send.at[k], rhs_recv.at[k], axis, -j))
            copies[-1].start()
        return copies

    def factors(axis, own, into, weights, copies):
        for copy in copies:
            copy.wait_recv()
        nodes = [tuple(own[k] for k in range(3))] + [tuple(into[j, k] for k in range(3)) for j in range(sizes[axis] - 1)]
        for k, value in enumerate(ring_factors(nodes)):
            weights[k] = value

    def solve(axis, own, into, weight, copies):
        for copy in copies:
            copy.wait_recv()
        pairs = [(own[0], own[1])] + [(into[j, 0], into[j, 1]) for j in range(sizes[axis] - 1)]
        return ring_apply(weight, pairs)

    halves = [slice(2 * c, 2 * c + 2) for c in range(2)]
    sent_x = []
    for c, at in enumerate(halves):

        def right_x(i, v, after, below):
            flux = scale[0] * (cx[i, at] * (after - v))
            right = (flux - below) + work1[i, at] - dec[i, at] * v * (1.0 + v * v) + forcing
            return right, flux

        def forward_x(i, carry):
            v, below, y, load = carry
            after = vx[i + 1, at]
            right, flux = right_x(i, v, after, below)
            y = right + ax[i - 1, at] * y
            work3[i, at] = y
            return after, flux, y, load + bx[i, at] * y

        v0, v1, v2 = vx[0, at], vx[1, at], vx[2, at]
        load, flux = right_x(0, v0, v1, 0.0)
        y, flux = right_x(1, v1, v2, flux)
        work3[1, at] = y
        v, below, y, load = rows_loop(2, 29, 1, forward_x, (v2, flux, y, load + bx[1, at] * y), 32)
        right, flux = right_x(31, v, halo_x[at], below)
        y = right + ax[30, at] * y
        work3[31, at] = y
        fx_own[c, 0] = load + bx[31, at] * y
        fx_own[c, 1] = ax[31, at] * y - flux
        sent_x.append(exchange(0, fx_own.at[c], fx_in.at[c], c * (sizes[0] - 1)))

    pl.semaphore_wait(known.at[1], len(near_z))
    greet(known.at[2], near_z)
    into_z(cz2, czz2, range(8))

    def matrix_row_z(i, carry):
        kz, lz, sz = carry
        rz[:, i], az[:, i], bz[:, i], lz, kz, sz = eliminate(1.0 + lz, kz, sz, half[2] * czz[:, i])
        return kz, lz, sz

    kz, lz, sz = rows_loop(1, 31, 1, matrix_row_z, (half[2] * czz[:, 0], zero, zero + 1.0), 32)
    coupling, left, excess = kz[0], sz[0], sz[1] + lz[0]
    for s in range(1, 4):
        inverse, alpha, beta, carried, coupling, left = eliminate(excess, coupling, left, kz[s])
        segz[0, s], segz[1, s], segz[2, s] = inverse, alpha, beta
        excess = carried + lz[s] + (sz[s + 1] if s < 3 else 0.0)
    mz_own[0], mz_own[1], mz_own[2] = coupling, left, excess

    pl.semaphore_wait(known.at[2], len(near_z))
    mats_z = send_matrix(2, mz_own, mz_in, first_z)
    factors(0, mx_own, mx_in, wx, mats_x)

    for c, at in enumerate(halves):
        node, after = solve(0, fx_own.at[c], fx_in.at[c], lambda k: wx[k, at], sent_x[c])

        def backward_x(i, u):
            u = (rx[i, at] * work3[i, at] + bx[i, at] * node) + ax[i, at] * u
            work1[i, at] = u
            return u

        rows_loop(31, 31, -1, backward_x, after, 32)
        work1[0, at] = node

    sent_y, first = [], 2 * (sizes[0] - 1)
    for c, at in enumerate(halves):

        def right_y(y):
            return jnp.stack([work1_2[pl.ds(xc * 256 + y, 8, stride=32), :] for xc in (2 * c, 2 * c + 1)])

        def forward_y(i, carry):
            y, load = carry
            y = right_y(i) + ay[at, i - 1] * y
            work2[at, i] = y
            return y, load + by[at, i] * y

        y = right_y(1)
        work2[at, 1] = y
        y, load = rows_loop(2, 30, 1, forward_y, (y, right_y(0) + by[at, 1] * y), 32)
        fy_own[c, 0] = load
        fy_own[c, 1] = ay[at, 31] * y
        sent_y.append(exchange(1, fy_own.at[c], fy_in.at[c], first))
        first += sizes[1] - 1

    factors(1, my_own, my_in, wy, mats_y)
    factors(2, mz_own, mz_in, wz, mats_z)

    zwork = work3.reshape(4, 32, 8, 128)
    zwork2 = work3.reshape(1024, 128)
    for c, at in enumerate(halves):
        node, after = solve(1, fy_own.at[c], fy_in.at[c], lambda k: wy[k, at], sent_y[c])

        def store_half(y, value):
            for m in range(2):
                work1_2[pl.ds((2 * c + m) * 256 + y, 8, stride=32), :] = value[m]

        def backward_y(i, u):
            u = (ry[at, i] * work2[at, i] + by[at, i] * node) + ay[at, i] * u
            store_half(i, u)
            return u

        rows_loop(31, 31, -1, backward_y, after, 32)
        store_half(0, node)
        into_z(work1_2, zwork2, range(4 * c, 4 * c + 4))

    def forward_z(i, carry):
        y, load = carry
        y = zwork[:, i] + az[:, i - 1] * y
        work2[:, i] = y
        return y, load + bz[:, i] * y

    y = zwork[:, 1]
    work2[:, 1] = y
    y, load = rows_loop(2, 30, 1, forward_z, (y, zwork[:, 0] + bz[:, 1] * y), 32)
    carried = az[:, 31] * y
    ys, left = [None], load[0]
    for s in range(1, 4):
        y = load[s] + carried[s - 1]
        if s > 1:
            y = y + segz[1, s - 1] * ys[-1]
        ys.append(y)
        left = left + segz[2, s] * y
    fz_own[0] = left
    fz_own[1] = carried[3] + segz[1, 3] * ys[3]

    sent_z = exchange(2, fz_own, fz_in, first)
    node, after = solve(2, fz_own, fz_in, lambda k: wz[k], sent_z)
    ends_z = [after]
    for s in (3, 2, 1):
        ends_z.insert(0, (segz[0, s] * ys[s] + segz[2, s] * node) + segz[1, s] * ends_z[0])
    starts_z = jnp.stack([node] + ends_z[:3])

    def backward_z(i, u):
        u = (rz[:, i] * work2[:, i] + bz[:, i] * starts_z) + az[:, i] * u
        zwork[:, i] = u
        return u

    rows_loop(31, 31, -1, backward_z, jnp.stack(ends_z), 32)
    zwork[:, 0] = starts_z

    for b in range(8):
        at = pl.ds(128 * b, 128)
        out2[at, :] = vx2[at, :] + zwork2[pl.ds(b, 128, stride=8), :].T
    for copy in mats_x + mats_y + mats_z + sum(sent_x, []) + sum(sent_y, []) + sent_z:
        copy.wait_send()


def on_device(sizes, density, conductance, decay_rate, diffusion_numbers, plane_offset):
    nx, ny, nz = sizes
    grid = (32, 4, 8, 128)
    lines = (4, 32, 8, 128)
    one = (4, 8, 128)
    two = (2, 8, 128)
    peers = nx + ny + nz - 3
    vmem = lambda *shape: pltpu.VMEM(shape, F32)
    dma = lambda n: pltpu.SemaphoreType.DMA((n,))
    operands = (
        diffusion_numbers,
        plane_offset,
        density.reshape(grid),
        conductance.reshape((3,) + grid),
        decay_rate.reshape(grid),
    )
    updated = pl.pallas_call(
        functools.partial(kernel, sizes),
        out_shape=jax.ShapeDtypeStruct(grid, F32),
        in_specs=[pl.BlockSpec(memory_space=pl.ANY)] * len(operands),
        out_specs=pl.BlockSpec(memory_space=pltpu.VMEM),
        scratch_shapes=[pltpu.SMEM((3,), F32), pltpu.SMEM((1,), jnp.int32)]
        + [vmem(*grid)] * 5
        + [vmem(*lines)] * 3
        + [vmem(*grid)] * 3
        + [vmem(*lines)] * 6
        + [vmem(3, 4, 8, 128)]
        + [vmem(2 * nx - 1, *one), vmem(2 * ny - 1, *one), vmem(2 * nz - 1, 8, 128)]
        + [vmem(*grid), vmem(*lines), vmem(*grid)]
        + [vmem(*one), vmem(3, 32, 128), vmem(3, 8, 128), vmem(3, 8, 128), vmem(128, 128), vmem(16, 128)]
        + [vmem(3, *one), vmem(3, *one), vmem(3, 8, 128)]
        + [vmem(nx - 1, 3, *one), vmem(ny - 1, 3, *one), vmem(nz - 1, 3, 8, 128)]
        + [vmem(2, 2, *two), vmem(2, 2, *two), vmem(2, 8, 128)]
        + [vmem(2, nx - 1, 2, *two), vmem(2, ny - 1, 2, *two), vmem(nz - 1, 2, 8, 128)]
        + [dma(7), dma(7), dma(7), dma(peers), dma(peers), dma(2 * peers), dma(2 * peers), pltpu.SemaphoreType.REGULAR((3,))],
        compiler_params=pltpu.CompilerParams(collective_id=0, has_side_effects=True, vmem_limit_bytes=40 * 1024 * 1024),
        name="adi_step",
    )(*(x if x.size == 1 else pltpu.with_memory_space_constraint(x, pltpu.MemorySpace.HBM) for x in operands))
    return updated.reshape(density.shape)


def solution(mesh):
    sizes = tuple(mesh.shape[a] for a in AXES)
    placed = (P("gx", "gy", "gz"), P(None, "gx", "gy", "gz"), P("gx", "gy", "gz"), P(), P())
    return jax.shard_map(
        functools.partial(on_device, sizes), mesh=mesh, in_specs=placed, out_specs=P("gx", "gy", "gz"), check_vma=False
    )
```
